32 devices in a mesh: groups: 2 (over y), gx: 4 (over z), gy: 2 (over x), gz: 2 (over core).
Axes of the slice: x: 2, y: 2, z: 4, core: 2. Of those that a mesh axis runs over, the one named last changes fastest.
Arguments:
- features: bfloat16 [32, 8, 32, 128], P(('groups', 'gx'), 'gy', 'gz'), parts along dimension 0, may hold values from -6 to 6
- scales: bfloat16 [32, 8, 32, 128], P(('groups', 'gx'), 'gy', 'gz'), parts along dimension 0, may hold values from 0.29882812 to 3
- occupancy: int32 [8, 2, 8], P(('groups', 'gx'), 'gy', 'gz'), parts along dimension 0, may hold values 0 or 1
- kernel: bfloat16 [62, 128, 128], replicated, may hold values from -0.0625 to 0.0625
- gamma: float32 [128, 128], replicated, may hold values from 0 to 0.015625
- beta: float32 [128], replicated, may hold values from 0.5 to 2
Outputs:
- grad_features: bfloat16 [32, 8, 32, 128], P(('groups', 'gx'), 'gy', 'gz'), parts along dimension 0
- grad_kernel: float32 [2031616], P(('groups', 'gx', 'gy', 'gz')), parts along dimension 0
- grad_gamma: float32 [256, 128], P('groups'), parts along dimension 0
- grad_beta: float32 [256], P('groups'), parts along dimension 0
The draws below stay inside these ranges and needn't reach their ends.
There are 2 independent parts, one for each index of `groups`. The reference program is written for one: setup_inputs(seed, part) draws one part's arguments, and reference() takes and returns one part's arrays. A program takes and returns all parts, laid end to end along the dimension named above; an argument that names none is the same for every part. Nothing has to cross between parts.
All inputs are finite; a program needn't handle non-finite values. No bound on the sum of `occupancy` on one device may be relied on, other than what follows from the above.
Results may differ from the reference program's by a relative error of at most 0.0039.
The reference program's roundings to bfloat16 on the way (of `latent` and `mean_grad`) count: a program that leaves them out, or rounds other values in their place, can miss the bound.
Values may be sent and summed in bfloat16 or wider, within the bound.
No kernel may reach another device: no remote copies, remote signals or barrier semaphores. Data moves between devices by JAX's collectives and lax.ppermute only.
A program may use at most 64 MiB of HBM per device.

```python
import math
import jax
import jax.numpy as jnp
from jax import lax

C = 128
TAPS = 62
OB = 4
NX = 16
NY = 8
NZ = 32
BLOCK = 256


def place_ends(drawn, own_key, low, high):
    spot = [jax.random.randint(jax.random.fold_in(own_key, axis), (), 0, length) for axis, length in enumerate(drawn.shape)]
    main_axis = drawn.shape.index(max(drawn.shape))
    neighbour = spot[:main_axis] + [(spot[main_axis] + 1) % drawn.shape[main_axis]] + spot[main_axis + 1:]
    return drawn.at[tuple(spot)].set(low).at[tuple(neighbour)].set(high)


def block_levels(stream_key, shape, pieces, smallest, high):
    gain = 1.0
    for axis_at, blocks in pieces:
        heights = jax.random.uniform(jax.random.fold_in(jax.random.fold_in(stream_key, 6), axis_at), (blocks,), jnp.float32, smallest / len(pieces), high / len(pieces))
        gain = gain * jnp.repeat(jnp.exp(heights), shape[axis_at] // blocks).reshape((-1,) + (1,) * (len(shape) - 1 - axis_at))
    return gain


def scatter_about(stream_key, shape, width, most, cuts=(), kind=jnp.bfloat16):
    values = jax.random.normal(stream_key, shape, jnp.float32) * width
    if len(cuts) > 0:
        values = block_levels(stream_key, shape, cuts, -0.22, 0.18) * values
    return jnp.clip(values, min=-most, max=most).astype(kind)


def setup_inputs(seed: int = 0, part: int = 0) -> dict:
    keys = jax.random.split(jax.random.key(seed), 7)
    part_keys = jax.random.split(jax.random.fold_in(keys[6], part), 7)
    features = scatter_about(part_keys[0], (NX, NY, NZ, C), 1.0, 6.0, ((0, 4), (1, 2), (2, 2)))
    scales = jnp.clip(jnp.exp(math.log(3.0) - 2.306499 * jax.random.uniform(part_keys[1], (NX, NY, NZ, C), jnp.float32) ** block_levels(part_keys[1], (NX, NY, NZ, C), ((0, 4), (1, 2), (2, 2)), -0.2, 0.2)), 0.29882812, 3.0).astype(jnp.bfloat16)
    occupancy = place_ends((jax.random.randint(part_keys[2], (NX // OB, NY // OB, NZ // OB), 0, 4) < 3).astype(jnp.int32), jax.random.fold_in(part_keys[2], 1), 0, 1)
    kernel = scatter_about(keys[3], (TAPS, C, C), (TAPS * C) ** -0.5, 0.0625)
    gamma = jnp.clip(jax.random.uniform(keys[4], (C, C), jnp.float32, 0.0, 0.015625), 0.0, 0.015625)
    beta = jnp.clip(jnp.exp(jax.random.uniform(keys[5], (C,), jnp.float32, math.log(0.5), math.log(2.0))), 0.5, 2.0)
    return dict(features=features, scales=scales, occupancy=occupancy, kernel=kernel, gamma=gamma, beta=beta)


def causal_offsets():
    result = []
    for along_x in range(-2, 3):
        for along_y in range(-2, 3):
            for along_z in range(-2, 3):
                if (along_x, along_y, along_z) < (0, 0, 0):
                    result.append((along_x, along_y, along_z))
    return result

def reference(features, scales, occupancy, kernel, gamma, beta):
    feats = features.astype(jnp.float32).reshape(-1, C)
    grown = jnp.repeat(jnp.repeat(jnp.repeat(occupancy, OB, 0), OB, 1), OB, 2)
    occupied = grown.reshape(-1, 1).astype(jnp.float32)
    energy = beta[None, :] + jnp.dot(feats * feats, gamma, precision=lax.Precision.HIGHEST, preferred_element_type=jnp.float32)
    inv_root = lax.rsqrt(energy)
    latent = (occupied * feats * inv_root).astype(jnp.bfloat16)
    latent_grid = latent.reshape(NX, NY, NZ, C)
    padded = jnp.pad(latent_grid, ((2, 2), (2, 2), (2, 2), (0, 0)))
    offsets = causal_offsets()
    mean = jnp.zeros((NX * NY * NZ, C), jnp.float32)
    for number, offset in enumerate(offsets):
        window = padded[2 + offset[0]:2 + offset[0] + NX, 2 + offset[1]:2 + offset[1] + NY, 2 + offset[2]:2 + offset[2] + NZ]
        mean = mean + jnp.dot(window.reshape(-1, C), kernel[number], preferred_element_type=jnp.float32)
    latent_f = latent.astype(jnp.float32)
    scale_f = scales.astype(jnp.float32).reshape(-1, C)
    inverse = 1.0 / (scale_f * scale_f)
    mean_grad = (occupied * (mean - latent_f) * inverse).astype(jnp.bfloat16)
    grad_pad = jnp.pad(mean_grad.reshape(NX, NY, NZ, C), ((2, 2), (2, 2), (2, 2), (0, 0)))
    context_grad = jnp.zeros((NX * NY * NZ, C), jnp.float32)
    kernel_terms = []
    for number, offset in enumerate(offsets):
        back = grad_pad[2 - offset[0]:2 - offset[0] + NX, 2 - offset[1]:2 - offset[1] + NY, 2 - offset[2]:2 - offset[2] + NZ]
        context_grad = context_grad + jnp.dot(back.reshape(-1, C), kernel[number].T, preferred_element_type=jnp.float32)
        window = padded[2 + offset[0]:2 + offset[0] + NX, 2 + offset[1]:2 + offset[1] + NY, 2 + offset[2]:2 + offset[2] + NZ]
        kernel_terms.append(jnp.dot(window.reshape(-1, C).T, mean_grad, preferred_element_type=jnp.float32))
    latent_grad = occupied * (context_grad + (latent_f - mean) * inverse)
    weighted = latent_grad * feats * inv_root * inv_root * inv_root
    coupled = jnp.dot(weighted, gamma.T, precision=lax.Precision.HIGHEST, preferred_element_type=jnp.float32)
    grad_features = (latent_grad * inv_root - feats * coupled).astype(jnp.bfloat16).reshape(NX, NY, NZ, C)
    grad_kernel = jnp.stack(kernel_terms).reshape(-1) / BLOCK
    factor = 0.5 / math.sqrt(BLOCK)
    grad_gamma = -factor * jnp.dot((feats * feats).T, weighted, precision=lax.Precision.HIGHEST, preferred_element_type=jnp.float32)
    grad_beta = -factor * lax.optimization_barrier(jnp.sum(weighted, axis=0))
    return (grad_features, grad_kernel, grad_gamma, grad_beta)
```

```python
import math

import jax
import jax.numpy as jnp
from jax import lax
from jax.sharding import PartitionSpec as P

OB = 4


def padded_2(shard, sides, width):
    for axis, dim in sides:
        size, length = (lax.axis_size(axis), shard.shape[dim])
        up = [(i, (i + 1) % size) for i in range(size - 1)]
        down = [(j, i) for i, j in up]
        last = lax.slice_in_dim(shard, length - width, length, axis=dim)
        leading = lax.slice_in_dim(shard, 0, width, axis=dim)
        before = lax.ppermute(last, axis, up)
        after = lax.ppermute(leading, axis, down)
        shard = jnp.concatenate([before, shard, after], axis=dim)
    return shard


def from_behind(value, axis, steps):
    count = lax.axis_size(axis)
    leading, last = (max(0, -steps), min(count, count - steps))
    return lax.ppermute(value, axis, [(source, source + steps) for source in range(leading, last)])


def causal_offsets():
    result = []
    for along_x in range(-2, 3):
        for along_y in range(-2, 3):
            for along_z in range(-2, 3):
                if (along_x, along_y, along_z) < (0, 0, 0):
                    result.append((along_x, along_y, along_z))
    return result


def tap_groups():
    groups = []
    for number, offset in enumerate(causal_offsets()):
        if groups and groups[-1][0] == offset[0] and (groups[-1][1] == offset[1]):
            groups[-1][3] += 1
        else:
            groups.append([offset[0], offset[1], offset[2], 1, number])
    return groups


def expand_blocks(occupancy, edge):
    blocks_x, blocks_y, blocks_z = occupancy.shape
    grown = jnp.broadcast_to(
        occupancy[:, None, :, None, :, None], (blocks_x, edge, blocks_y, edge, blocks_z, edge)
    )
    return grown.reshape(-1, 1).astype(jnp.float32)


def forward_patch(padded, along_x, along_y, start_z, count, extent):
    size_x, size_y, size_z = extent
    pieces = [
        padded[
            2 + along_x : 2 + along_x + size_x,
            2 + along_y : 2 + along_y + size_y,
            2 + along_z : 2 + along_z + size_z,
        ]
        for along_z in range(start_z, start_z + count)
    ]
    return jnp.concatenate(pieces, axis=3).reshape(size_x * size_y * size_z, -1)


def context_mean(padded, kernel, extent):
    channels = kernel.shape[1]
    total = jnp.zeros((extent[0] * extent[1] * extent[2], channels), jnp.float32)
    for along_x, along_y, start_z, count, first_tap in tap_groups():
        patch = forward_patch(padded, along_x, along_y, start_z, count, extent)
        weights = kernel[first_tap : first_tap + count].reshape(count * channels, channels)
        total = total + jnp.dot(patch, weights, preferred_element_type=jnp.float32)
    return total


def context_transposed(padded, kernel, extent):
    size_x, size_y, size_z = extent
    channels = kernel.shape[1]
    total = jnp.zeros((size_x * size_y * size_z, channels), jnp.float32)
    for along_x, along_y, start_z, count, first_tap in tap_groups():
        pieces = [
            padded[
                -along_x : -along_x + size_x,
                2 - along_y : 2 - along_y + size_y,
                2 - along_z : 2 - along_z + size_z,
            ]
            for along_z in range(start_z, start_z + count)
        ]
        patch = jnp.concatenate(pieces, axis=3).reshape(size_x * size_y * size_z, -1)
        weights = jnp.transpose(kernel[first_tap : first_tap + count], (0, 2, 1)).reshape(
            count * channels, channels
        )
        total = total + jnp.dot(patch, weights, preferred_element_type=jnp.float32)
    return total


def kernel_terms(padded, mean_grad, extent):
    terms = []
    for along_x, along_y, start_z, count, first_tap in tap_groups():
        patch = forward_patch(padded, along_x, along_y, start_z, count, extent)
        terms.append(
            lax.dot_general(
                patch, mean_grad, (((0,), (0,)), ((), ())), preferred_element_type=jnp.float32
            )
        )
    return jnp.concatenate(terms, axis=0).reshape(-1)


def lower_sides_first(latent):
    widened = padded_2(latent, (("gy", 1), ("gz", 2)), 2)
    below = from_behind(widened[-2:], "gx", 1)
    return jnp.concatenate([below, widened], axis=0)


def upper_sides_first(grads):
    widened = padded_2(grads, (("gy", 1), ("gz", 2)), 2)
    above = from_behind(widened[:2], "gx", -1)
    return jnp.concatenate([widened, above], axis=0)


def swapped(value, axis, partner):
    count = lax.axis_size(axis)
    return lax.ppermute(value, axis, [(i, partner(i)) for i in range(count)])


def gathered(shard, axis, dim):
    count = lax.axis_size(axis)
    place = lax.axis_index(axis)
    if count == 2:
        other = swapped(shard, axis, lambda i: 1 - i)
        orders = ((shard, other), (other, shard))
    elif count == 4:
        mirror = swapped(shard, axis, lambda i: 3 - i)
        pair = swapped(jnp.stack([shard, mirror]), axis, lambda i: i ^ 1)
        near, far = pair[0], pair[1]
        orders = (
            (shard, near, far, mirror),
            (near, shard, mirror, far),
            (far, mirror, shard, near),
            (mirror, far, near, shard),
        )
    else:
        return lax.all_gather(shard, axis, axis=dim, tiled=True)
    return lax.select_n(place, *[jnp.concatenate(order, axis=dim) for order in orders])


def whole_slab(block):
    for axis, dim in (("gx", 0), ("gy", 1), ("gz", 2)):
        block = gathered(block, axis, dim)
    return block


def summed(value):
    for axis in ("gz", "gy", "gx"):
        count = lax.axis_size(axis)
        if count & (count - 1):
            value = lax.psum(value, axis)
            continue
        step = 1
        while step < count:
            value = value + swapped(value, axis, lambda i: i ^ step)
            step *= 2
    return value


def own_kernel_rows(latent_grid, grad_grid):
    slab, grads = whole_slab(latent_grid), whole_slab(grad_grid)
    size_x, size_y, size_z, channels = slab.shape
    offsets = causal_offsets()
    devices = lax.axis_size(("gx", "gy", "gz"))
    rows = len(offsets) * channels // devices
    spanned = max(-(-((d * rows) % channels + rows) // channels) for d in range(devices))
    first_row = lax.axis_index(("gx", "gy", "gz")) * rows
    first_tap = jnp.minimum(first_row // channels, len(offsets) - spanned)
    table = jnp.array(offsets, jnp.int32)
    padded = jnp.pad(slab, ((2, 0), (2, 2), (2, 2), (0, 0)))
    pieces = []
    for number in range(spanned):
        shift = lax.dynamic_index_in_dim(table, first_tap + number, keepdims=False)
        pieces.append(
            lax.dynamic_slice(
                padded, (2 + shift[0], 2 + shift[1], 2 + shift[2], 0), (size_x, size_y, size_z, channels)
            ).reshape(-1, channels)
        )
    product = lax.dot_general(
        jnp.concatenate(pieces, axis=1),
        grads.reshape(-1, channels),
        (((0,), (0,)), ((), ())),
        preferred_element_type=jnp.float32,
    )
    return lax.dynamic_slice(
        product, (first_row - first_tap * channels, 0), (rows, channels)
    ).reshape(-1)


def local(features, scales, occupancy, kernel, gamma, beta):
    size_x, size_y, size_z, channels = features.shape
    extent = (size_x, size_y, size_z)
    voxels = size_x * size_y * size_z
    feats = features.astype(jnp.float32).reshape(voxels, channels)
    occupied = expand_blocks(occupancy, OB)
    energy = beta[None, :] + jnp.dot(
        feats * feats, gamma, precision=lax.Precision.HIGHEST, preferred_element_type=jnp.float32
    )
    inv_root = lax.rsqrt(energy)
    latent = (occupied * feats * inv_root).astype(jnp.bfloat16)
    latent_grid = latent.reshape(size_x, size_y, size_z, channels)
    padded = lower_sides_first(latent_grid)
    mean = context_mean(padded, kernel, extent)
    latent_f = latent.astype(jnp.float32)
    scale_f = scales.astype(jnp.float32).reshape(voxels, channels)
    inverse = 1.0 / (scale_f * scale_f)
    mean_grad = (occupied * (mean - latent_f) * inverse).astype(jnp.bfloat16)
    grad_grid = mean_grad.reshape(size_x, size_y, size_z, channels)
    grad_pad = upper_sides_first(grad_grid)
    context_grad = context_transposed(grad_pad, kernel, extent)
    latent_grad = occupied * (context_grad + (latent_f - mean) * inverse)
    weighted = latent_grad * feats * inv_root * inv_root * inv_root
    coupled = jnp.dot(
        weighted, gamma.T, precision=lax.Precision.HIGHEST, preferred_element_type=jnp.float32
    )
    grad_features = (
        (latent_grad * inv_root - feats * coupled)
        .astype(jnp.bfloat16)
        .reshape(size_x, size_y, size_z, channels)
    )
    devices = lax.axis_size(("gx", "gy", "gz"))
    fits = devices * voxels <= 16384 and (62 * channels) % devices == 0
    if fits:
        grad_kernel = own_kernel_rows(latent_grid, grad_grid) / voxels
    else:
        grad_kernel = lax.psum_scatter(
            kernel_terms(padded, mean_grad, extent) / voxels,
            ("gx", "gy", "gz"),
            scatter_dimension=0,
            tiled=True,
        )
    factor = 0.5 / math.sqrt(voxels)
    gamma_local = -factor * jnp.dot(
        (feats * feats).T,
        weighted,
        precision=lax.Precision.HIGHEST,
        preferred_element_type=jnp.float32,
    )
    beta_local = -factor * jnp.sum(weighted, axis=0)
    both = summed(jnp.concatenate([gamma_local, jnp.broadcast_to(beta_local, (8, channels))], axis=0))
    grad_gamma, grad_beta = both[:channels], both[channels]
    return (grad_features, grad_kernel, grad_gamma, grad_beta)


def solution(mesh):
    return jax.shard_map(
        local,
        mesh=mesh,
        in_specs=(
            P(("groups", "gx"), "gy", "gz", None),
            P(("groups", "gx"), "gy", "gz", None),
            P(("groups", "gx"), "gy", "gz"),
            P(),
            P(),
            P(),
        ),
        out_specs=(
            P(("groups", "gx"), "gy", "gz", None),
            P(("groups", "gx", "gy", "gz")),
            P("groups", None),
            P("groups"),
        ),
        check_vma=False,
    )
```

```python
import functools
import math

import jax
import jax.numpy as jnp
from jax import lax
from jax.experimental import pallas as pl
from jax.experimental.pallas import tpu as pltpu
from jax.sharding import PartitionSpec as P

OB = 4


def padded_2(shard, sides, width):
    for axis, dim in sides:
        size, length = (lax.axis_size(axis), shard.shape[dim])
        up = [(i, (i + 1) % size) for i in range(size - 1)]
        down = [(j, i) for i, j in up]
        last = lax.slice_in_dim(shard, length - width, length, axis=dim)
        leading = lax.slice_in_dim(shard, 0, width, axis=dim)
        before = lax.ppermute(last, axis, up)
        after = lax.ppermute(leading, axis, down)
        shard = jnp.concatenate([before, shard, after], axis=dim)
    return shard


def from_behind(value, axis, steps):
    count = lax.axis_size(axis)
    leading, last = (max(0, -steps), min(count, count - steps))
    return lax.ppermute(value, axis, [(source, source + steps) for source in range(leading, last)])


def causal_offsets():
    result = []
    for along_x in range(-2, 3):
        for along_y in range(-2, 3):
            for along_z in range(-2, 3):
                if (along_x, along_y, along_z) < (0, 0, 0):
                    result.append((along_x, along_y, along_z))
    return result


def tap_groups():
    groups = []
    for number, offset in enumerate(causal_offsets()):
        if groups and groups[-1][0] == offset[0] and (groups[-1][1] == offset[1]):
            groups[-1][3] += 1
        else:
            groups.append([offset[0], offset[1], offset[2], 1, number])
    return groups


def expand_blocks(occupancy, edge):
    blocks_x, blocks_y, blocks_z = occupancy.shape
    grown = jnp.broadcast_to(
        occupancy[:, None, :, None, :, None], (blocks_x, edge, blocks_y, edge, blocks_z, edge)
    )
    return grown.reshape(-1, 1).astype(jnp.float32)


def forward_patch(padded, along_x, along_y, start_z, count, extent):
    size_x, size_y, size_z = extent
    pieces = [
        padded[
            2 + along_x : 2 + along_x + size_x,
            2 + along_y : 2 + along_y + size_y,
            2 + along_z : 2 + along_z + size_z,
        ]
        for along_z in range(start_z, start_z + count)
    ]
    return jnp.concatenate(pieces, axis=3).reshape(size_x * size_y * size_z, -1)


def context_mean(padded, kernel, extent):
    channels = kernel.shape[1]
    total = jnp.zeros((extent[0] * extent[1] * extent[2], channels), jnp.float32)
    for along_x, along_y, start_z, count, first_tap in tap_groups():
        patch = forward_patch(padded, along_x, along_y, start_z, count, extent)
        weights = kernel[first_tap : first_tap + count].reshape(count * channels, channels)
        total = total + jnp.dot(patch, weights, preferred_element_type=jnp.float32)
    return total


def context_transposed(padded, kernel, extent):
    size_x, size_y, size_z = extent
    channels = kernel.shape[1]
    total = jnp.zeros((size_x * size_y * size_z, channels), jnp.float32)
    for along_x, along_y, start_z, count, first_tap in tap_groups():
        pieces = [
            padded[
                -along_x : -along_x + size_x,
                2 - along_y : 2 - along_y + size_y,
                2 - along_z : 2 - along_z + size_z,
            ]
            for along_z in range(start_z, start_z + count)
        ]
        patch = jnp.concatenate(pieces, axis=3).reshape(size_x * size_y * size_z, -1)
        weights = jnp.transpose(kernel[first_tap : first_tap + count], (0, 2, 1)).reshape(
            count * channels, channels
        )
        total = total + jnp.dot(patch, weights, preferred_element_type=jnp.float32)
    return total


def kernel_terms(padded, mean_grad, extent):
    terms = []
    for along_x, along_y, start_z, count, first_tap in tap_groups():
        patch = forward_patch(padded, along_x, along_y, start_z, count, extent)
        terms.append(
            lax.dot_general(
                patch, mean_grad, (((0,), (0,)), ((), ())), preferred_element_type=jnp.float32
            )
        )
    return jnp.concatenate(terms, axis=0).reshape(-1)


def lower_sides_first(latent):
    widened = padded_2(latent, (("gy", 1), ("gz", 2)), 2)
    below = from_behind(widened[-2:], "gx", 1)
    return jnp.concatenate([below, widened], axis=0)


def upper_sides_first(grads):
    widened = padded_2(grads, (("gy", 1), ("gz", 2)), 2)
    above = from_behind(widened[:2], "gx", -1)
    return jnp.concatenate([widened, above], axis=0)


def local(features, scales, occupancy, kernel, gamma, beta):
    size_x, size_y, size_z, channels = features.shape
    extent = (size_x, size_y, size_z)
    voxels = size_x * size_y * size_z
    feats = features.astype(jnp.float32).reshape(voxels, channels)
    occupied = expand_blocks(occupancy, OB)
    energy = beta[None, :] + jnp.dot(
        feats * feats, gamma, precision=lax.Precision.HIGHEST, preferred_element_type=jnp.float32
    )
    inv_root = lax.rsqrt(energy)
    latent = (occupied * feats * inv_root).astype(jnp.bfloat16)
    latent_grid = latent.reshape(size_x, size_y, size_z, channels)
    padded = lower_sides_first(latent_grid)
    mean = context_mean(padded, kernel, extent)
    latent_f = latent.astype(jnp.float32)
    scale_f = scales.astype(jnp.float32).reshape(voxels, channels)
    inverse = 1.0 / (scale_f * scale_f)
    mean_grad = (occupied * (mean - latent_f) * inverse).astype(jnp.bfloat16)
    grad_grid = mean_grad.reshape(size_x, size_y, size_z, channels)
    grad_pad = upper_sides_first(grad_grid)
    context_grad = context_transposed(grad_pad, kernel, extent)
    latent_grad = occupied * (context_grad + (latent_f - mean) * inverse)
    weighted = latent_grad * feats * inv_root * inv_root * inv_root
    coupled = jnp.dot(
        weighted, gamma.T, precision=lax.Precision.HIGHEST, preferred_element_type=jnp.float32
    )
    grad_features = (
        (latent_grad * inv_root - feats * coupled)
        .astype(jnp.bfloat16)
        .reshape(size_x, size_y, size_z, channels)
    )
    kernel_local = kernel_terms(padded, mean_grad, extent) / voxels
    grad_kernel = lax.psum_scatter(
        kernel_local, ("gx", "gy", "gz"), scatter_dimension=0, tiled=True
    )
    factor = 0.5 / math.sqrt(voxels)
    gamma_local = -factor * jnp.dot(
        (feats * feats).T,
        weighted,
        precision=lax.Precision.HIGHEST,
        preferred_element_type=jnp.float32,
    )
    beta_local = -factor * jnp.sum(weighted, axis=0)
    grad_gamma, grad_beta = lax.psum((gamma_local, beta_local), ("gx", "gy", "gz"))
    return (grad_features, grad_kernel, grad_gamma, grad_beta)


HIGHEST = lax.Precision.HIGHEST
F32 = jnp.float32
BF16 = jnp.bfloat16
EDGE = 8


def exchanged(value, axes, target):
    names = (axes,) if isinstance(axes, str) else axes
    sizes = [lax.axis_size(name) for name in names]
    places = [()]
    for size in sizes:
        places = [place + (i,) for place in places for i in range(size)]
    pairs = []
    for number, place in enumerate(places):
        goal = target(*place)
        if all(0 <= spot < size for spot, size in zip(goal, sizes)):
            flat = 0
            for spot, size in zip(goal, sizes):
                flat = flat * size + spot
            pairs.append((number, flat))
    return lax.ppermute(value, names if len(names) > 1 else names[0], pairs)


def sum_over(value):
    value = value + exchanged(value, "gz", lambda z: (1 - z,))
    value = value + exchanged(value, "gy", lambda y: (1 - y,))
    value = value + exchanged(value, "gx", lambda x: (x ^ 1,))
    return value + exchanged(value, "gx", lambda x: (3 - x,))


def occupied_rows(occupancy, extent, channels):
    size_x, size_y, size_z = extent
    level = lax.broadcasted_iota(jnp.int32, (size_z, channels), 0) // OB
    layers = []
    for bx in range(size_x // OB):
        lines = []
        for by in range(size_y // OB):
            column = jnp.zeros((size_z, channels), F32)
            for bz in range(size_z // OB):
                value = occupancy[bx, by, bz].astype(F32)
                column = jnp.where(level == bz, value, column)
            lines.append(jnp.broadcast_to(column[None, None], (OB, OB, size_z, channels)))
        layers.append(jnp.concatenate(lines, axis=1) if len(lines) > 1 else lines[0])
    mask = jnp.concatenate(layers, axis=0) if len(layers) > 1 else layers[0]
    return mask.reshape(size_x * size_y * size_z, channels)


def latent_kernel(features, occupancy, gamma, beta, latent, top, root):
    size_x, size_y, size_z, channels = features.shape
    feats = features[...].astype(F32).reshape(-1, channels)
    energy = beta[...] + jnp.dot(
        feats * feats, gamma[...], precision=HIGHEST, preferred_element_type=F32
    )
    inv_root = lax.rsqrt(energy)
    root[...] = inv_root
    occupied = occupied_rows(occupancy, features.shape[:3], channels)
    rounded = (occupied * feats * inv_root).astype(BF16).reshape(features.shape)
    latent[...] = rounded
    top[...] = rounded[size_x - 2 :]


def fill_wide(wide, own, side, layers, corner, own_z, side_z, layers_z, corner_z, at_own, at_layers):
    size_x, size_y, size_z, _ = own.shape
    first_y = lax.axis_index("gy") == 0
    first_z = lax.axis_index("gz") == 0
    to_y = jnp.where(first_y, 2 + size_y, 0)
    no_y = jnp.where(first_y, 0, 2 + size_y)
    from_y = jnp.where(first_y, 0, size_y - 2)
    after = EDGE + size_z

    def put(at_x, at_y, main, across):
        span = (pl.ds(at_x, main.shape[0]), pl.ds(at_y, main.shape[1]))
        wide[span + (pl.ds(EDGE, size_z),)] = main.astype(F32)
        across = across.astype(F32)
        wide[span + (pl.ds(0, EDGE),)] = jnp.where(first_z, 0.0, across[:, :, size_z - EDGE :])
        wide[span + (pl.ds(after, EDGE),)] = jnp.where(first_z, across[:, :, :EDGE], 0.0)

    put(at_own, 2, own[...], own_z[...])
    put(at_layers, 2, layers[...], layers_z[...])
    two = pl.ds(from_y, 2)
    put(at_own, to_y, side[:, two], side_z[:, two])
    put(at_layers, to_y, corner[:, two], corner_z[:, two])
    blank = (size_x + 2, 2) + wide.shape[2:]
    wide[:, pl.ds(no_y, 2)] = jnp.zeros(blank, F32)


def spread_shifts(wide, shifted, size_z, sign):
    channels = wide.shape[3]
    for number in range(5):
        start = EDGE + sign * (number - 2)
        shifted[:, :, :, number * channels : (number + 1) * channels] = wide[
            :, :, start : start + size_z, :
        ].astype(BF16)


def mean_kernel(
    own, side, layers, corner, own_z, side_z, layers_z, corner_z,
    kernel, scales, occupancy, grad, bottom, rest, wide, shifted,
):
    size_x, size_y, size_z, channels = own.shape
    fill_wide(wide, own, side, layers, corner, own_z, side_z, layers_z, corner_z, 2, 0)
    spread_shifts(wide, shifted, size_z, 1)
    total = jnp.zeros((size_x * size_y * size_z, channels), F32)
    for along_x, along_y, _, count, first_tap in tap_groups():
        patch = shifted[
            2 + along_x : 2 + along_x + size_x,
            2 + along_y : 2 + along_y + size_y,
            :,
            : count * channels,
        ].reshape(-1, count * channels)
        weights = kernel[first_tap : first_tap + count].reshape(count * channels, channels)
        total = total + jnp.dot(patch, weights, preferred_element_type=F32)
    scale = scales[...].astype(F32).reshape(-1, channels)
    inverse = 1.0 / (scale * scale)
    latent = own[...].astype(F32).reshape(-1, channels)
    difference = (total - latent) * inverse
    occupied = occupied_rows(occupancy, own.shape[:3], channels)
    rounded = (occupied * difference).astype(BF16).reshape(own.shape)
    grad[...] = rounded
    bottom[...] = rounded[:2]
    rest[...] = -difference


def feature_kernel(
    own, side, layers, corner, own_z, side_z, layers_z, corner_z,
    kernel, rest, root, features, gamma, occupancy, grad_features, sums, wide, shifted,
):
    size_x, size_y, size_z, channels = own.shape
    voxels = size_x * size_y * size_z
    fill_wide(wide, own, side, layers, corner, own_z, side_z, layers_z, corner_z, 0, size_x)
    spread_shifts(wide, shifted, size_z, -1)
    total = jnp.zeros((voxels, channels), F32)
    for along_x, along_y, _, count, first_tap in tap_groups():
        patch = shifted[
            -along_x : -along_x + size_x,
            2 - along_y : 2 - along_y + size_y,
            :,
            : count * channels,
        ].reshape(-1, count * channels)
        weights = jnp.concatenate([kernel[first_tap + k] for k in range(count)], axis=1)
        total = total + lax.dot_general(
            patch, weights, (((1,), (1,)), ((), ())), preferred_element_type=F32
        )
    occupied = occupied_rows(occupancy, own.shape[:3], channels)
    latent_grad = occupied * (total + rest[...])
    inv_root = root[...]
    feats = features[...].astype(F32).reshape(voxels, channels)
    weighted = latent_grad * feats * inv_root * inv_root * inv_root
    coupled = lax.dot_general(
        weighted, gamma[...], (((1,), (1,)), ((), ())), precision=HIGHEST, preferred_element_type=F32
    )
    grad_features[...] = (latent_grad * inv_root - feats * coupled).astype(BF16).reshape(features.shape)
    factor = 0.5 / math.sqrt(voxels)
    sums[:channels] = -factor * jnp.dot(
        (feats * feats).T, weighted, precision=HIGHEST, preferred_element_type=F32
    )
    ones = jnp.sum(weighted, axis=0, keepdims=True)
    sums[channels:] = -factor * jnp.broadcast_to(ones, (8, channels))


def share_kernel(spanned, rows, voxels, *refs):
    latent_parts, grad_parts = refs[:8], refs[8:16]
    share, wide, flat, turned, product = refs[16:]
    size_x, size_y, size_z, channels = latent_parts[0].shape
    gx, gy, gz = lax.axis_index("gx"), lax.axis_index("gy"), lax.axis_index("gz")
    all_x, all_y, all_z = wide.shape[0] - 2, wide.shape[1] - 4, wide.shape[2] - 2 * EDGE
    lines = (wide.shape[1], wide.shape[2], channels)
    for layer in range(2):
        wide[layer] = jnp.zeros(lines, F32)
    for start in (0, 2 + all_y):
        wide[2:, start : start + 2] = jnp.zeros((all_x, 2, wide.shape[2], channels), F32)
    for start in (0, EDGE + all_z):
        wide[2:, 2 : 2 + all_y, start : start + EDGE] = jnp.zeros((all_x, all_y, EDGE, channels), F32)

    def place(parts, store):
        for across_z in range(2):
            at_z = pl.multiple_of((gz if across_z == 0 else 1 - gz) * size_z, size_z)
            for across_y in range(2):
                at_y = (gy if across_y == 0 else 1 - gy) * size_y
                single, triple = parts[4 * across_z + 2 * across_y], parts[4 * across_z + 2 * across_y + 1]
                store(gx * size_x, at_y, at_z, single[...])
                for other in range(1, 4):
                    store((gx ^ other) * size_x, at_y, at_z, triple[other - 1])

    def store_latent(at_x, at_y, at_z, value):
        wide[
            pl.ds(2 + at_x, size_x), pl.ds(2 + at_y, size_y), pl.ds(pl.multiple_of(EDGE + at_z, EDGE), size_z)
        ] = value.astype(F32)

    def store_grad(at_x, at_y, at_z, value):
        flat[pl.ds(at_x, size_x), pl.ds(at_y, size_y), pl.ds(at_z, size_z)] = value

    place(latent_parts, store_latent)
    place(grad_parts, store_grad)
    turned[...] = flat[...].reshape(-1, channels).T
    first_row = ((gx * 2 + gy) * 2 + gz) * rows
    first_tap = jnp.minimum(first_row // channels, 62 - spanned)
    for level in range(5):
        number = lax.rem(level + 5 - lax.rem(first_tap, 5), 5)
        group = (first_tap + number) // 5
        along_x, along_y = group // 5, lax.rem(group, 5)
        start = EDGE + level - 2
        patch = wide[pl.ds(along_x, all_x), pl.ds(along_y, all_y), start : start + all_z]
        result = jnp.dot(
            turned[...], patch.astype(BF16).reshape(-1, channels), preferred_element_type=F32
        )
        product[pl.ds(pl.multiple_of(number * channels, channels), channels)] = result.T * (1.0 / voxels)
    offset = pl.multiple_of(first_row - first_tap * channels, 16)
    share[...] = product[pl.ds(offset, rows)]


def call(body, outs, scratch, smem, args):
    in_specs = [
        pl.BlockSpec(memory_space=pltpu.SMEM if n in smem else pltpu.VMEM) for n in range(len(args))
    ]
    return pl.pallas_call(
        body,
        out_shape=outs,
        in_specs=in_specs,
        out_specs=[pl.BlockSpec(memory_space=pltpu.VMEM)] * len(outs),
        scratch_shapes=scratch,
    )(*args)


def with_neighbours(block, layers, step):
    flip = lambda i: 1 - i
    side = exchanged(block, "gy", lambda y: (flip(y),))
    near = exchanged(layers, "gx", lambda x: (x + step,))
    corner = exchanged(layers, ("gx", "gy"), lambda x, y: (x + step, flip(y)))
    mine = (block, side, near, corner)
    return mine + tuple(exchanged(part, "gz", lambda z: (flip(z),)) for part in mine)


def whole_parts(parts):
    block, side, side_z, block_z = parts[0], parts[1], parts[5], parts[4]
    others = jnp.stack([exchanged(block, "gx", lambda x, k=k: (x ^ k,)) for k in (1, 2, 3)])
    others_y = exchanged(others, "gy", lambda y: (1 - y,))
    others_z = exchanged(others, "gz", lambda z: (1 - z,))
    others_yz = exchanged(others_y, "gz", lambda z: (1 - z,))
    return (block, others, side, others_y, block_z, others_z, side_z, others_yz)


def fast_local(features, scales, occupancy, kernel, gamma, beta):
    shape = features.shape
    size_x, size_y, size_z, channels = shape
    voxels = size_x * size_y * size_z
    struct = jax.ShapeDtypeStruct
    layers = struct((2,) + shape[1:], BF16)
    rows_f32 = struct((voxels, channels), F32)
    wide = pltpu.VMEM((size_x + 2, size_y + 4, size_z + 2 * EDGE, channels), F32)
    shifted = pltpu.VMEM((size_x + 2, size_y + 4, size_z, 5 * channels), BF16)
    latent, top, root = call(
        latent_kernel, [struct(shape, BF16), layers, rows_f32], [], (1,),
        (features, occupancy, gamma, beta.reshape(1, channels)),
    )
    latents = with_neighbours(latent, top, 1)
    grad, bottom, rest = call(
        mean_kernel, [struct(shape, BF16), layers, rows_f32], [wide, shifted], (10,),
        latents + (kernel, scales, occupancy),
    )
    grads = with_neighbours(grad, bottom, -1)
    grad_features, sums = call(
        feature_kernel, [struct(shape, BF16), struct((channels + 8, channels), F32)], [wide, shifted], (13,),
        grads + (kernel, rest, root, features, gamma, occupancy),
    )
    sums = sum_over(sums)
    devices = 16
    rows = 62 * channels // devices
    spanned = 5
    all_x, all_y, all_z = 4 * size_x, 2 * size_y, 2 * size_z
    share, = call(
        functools.partial(share_kernel, spanned, rows, voxels),
        [struct((rows, channels), F32)],
        [
            pltpu.VMEM((all_x + 2, all_y + 4, all_z + 2 * EDGE, channels), F32),
            pltpu.VMEM((all_x, all_y, all_z, channels), BF16),
            pltpu.VMEM((channels, all_x * all_y * all_z), BF16),
            pltpu.VMEM((spanned * channels, channels), F32),
        ],
        (),
        whole_parts(latents) + whole_parts(grads),
    )
    return grad_features, share.reshape(-1), sums[:channels], sums[channels]


def chosen(features, scales, occupancy, kernel, gamma, beta):
    sizes = tuple(lax.axis_size(axis) for axis in ("gx", "gy", "gz"))
    size_x, size_y, size_z, channels = features.shape
    small = size_x >= 2 and size_y >= 2 and size_z % 16 == 0 and size_x * size_y * size_z <= 1024
    if sizes == (4, 2, 2) and small and channels == 128:
        return fast_local(features, scales, occupancy, kernel, gamma, beta)
    return local(features, scales, occupancy, kernel, gamma, beta)


def solution(mesh):
    return jax.shard_map(
        chosen,
        mesh=mesh,
        in_specs=(
            P(("groups", "gx"), "gy", "gz", None),
            P(("groups", "gx"), "gy", "gz", None),
            P(("groups", "gx"), "gy", "gz"),
            P(),
            P(),
            P(),
        ),
        out_specs=(
            P(("groups", "gx"), "gy", "gz", None),
            P(("groups", "gx", "gy", "gz")),
            P("groups", None),
            P("groups"),
        ),
        check_vma=False,
    )
```

```python
import functools
import math

import jax
import jax.numpy as jnp
from jax import lax
from jax.experimental import pallas as pl
from jax.experimental.pallas import tpu as pltpu
from jax.sharding import PartitionSpec as P

OB = 4


def padded_2(shard, sides, width):
    for axis, dim in sides:
        size, length = (lax.axis_size(axis), shard.shape[dim])
        up = [(i, (i + 1) % size) for i in range(size - 1)]
        down = [(j, i) for i, j in up]
        last = lax.slice_in_dim(shard, length - width, length, axis=dim)
        leading = lax.slice_in_dim(shard, 0, width, axis=dim)
        before = lax.ppermute(last, axis, up)
        after = lax.ppermute(leading, axis, down)
        shard = jnp.concatenate([before, shard, after], axis=dim)
    return shard


def from_behind(value, axis, steps):
    count = lax.axis_size(axis)
    leading, last = (max(0, -steps), min(count, count - steps))
    return lax.ppermute(value, axis, [(source, source + steps) for source in range(leading, last)])


def causal_offsets():
    result = []
    for along_x in range(-2, 3):
        for along_y in range(-2, 3):
            for along_z in range(-2, 3):
                if (along_x, along_y, along_z) < (0, 0, 0):
                    result.append((along_x, along_y, along_z))
    return result


def tap_groups():
    groups = []
    for number, offset in enumerate(causal_offsets()):
        if groups and groups[-1][0] == offset[0] and (groups[-1][1] == offset[1]):
            groups[-1][3] += 1
        else:
            groups.append([offset[0], offset[1], offset[2], 1, number])
    return groups


def expand_blocks(occupancy, edge):
    blocks_x, blocks_y, blocks_z = occupancy.shape
    grown = jnp.broadcast_to(
        occupancy[:, None, :, None, :, None], (blocks_x, edge, blocks_y, edge, blocks_z, edge)
    )
    return grown.reshape(-1, 1).astype(jnp.float32)


def forward_patch(padded, along_x, along_y, start_z, count, extent):
    size_x, size_y, size_z = extent
    pieces = [
        padded[
            2 + along_x : 2 + along_x + size_x,
            2 + along_y : 2 + along_y + size_y,
            2 + along_z : 2 + along_z + size_z,
        ]
        for along_z in range(start_z, start_z + count)
    ]
    return jnp.concatenate(pieces, axis=3).reshape(size_x * size_y * size_z, -1)


def context_mean(padded, kernel, extent):
    channels = kernel.shape[1]
    total = jnp.zeros((extent[0] * extent[1] * extent[2], channels), jnp.float32)
    for along_x, along_y, start_z, count, first_tap in tap_groups():
        patch = forward_patch(padded, along_x, along_y, start_z, count, extent)
        weights = kernel[first_tap : first_tap + count].reshape(count * channels, channels)
        total = total + jnp.dot(patch, weights, preferred_element_type=jnp.float32)
    return total


def context_transposed(padded, kernel, extent):
    size_x, size_y, size_z = extent
    channels = kernel.shape[1]
    total = jnp.zeros((size_x * size_y * size_z, channels), jnp.float32)
    for along_x, along_y, start_z, count, first_tap in tap_groups():
        pieces = [
            padded[
                -along_x : -along_x + size_x,
                2 - along_y : 2 - along_y + size_y,
                2 - along_z : 2 - along_z + size_z,
            ]
            for along_z in range(start_z, start_z + count)
        ]
        patch = jnp.concatenate(pieces, axis=3).reshape(size_x * size_y * size_z, -1)
        weights = jnp.transpose(kernel[first_tap : first_tap + count], (0, 2, 1)).reshape(
            count * channels, channels
        )
        total = total + jnp.dot(patch, weights, preferred_element_type=jnp.float32)
    return total


def kernel_terms(padded, mean_grad, extent):
    terms = []
    for along_x, along_y, start_z, count, first_tap in tap_groups():
        patch = forward_patch(padded, along_x, along_y, start_z, count, extent)
        terms.append(
            lax.dot_general(
                patch, mean_grad, (((0,), (0,)), ((), ())), preferred_element_type=jnp.float32
            )
        )
    return jnp.concatenate(terms, axis=0).reshape(-1)


def lower_sides_first(latent):
    widened = padded_2(latent, (("gy", 1), ("gz", 2)), 2)
    below = from_behind(widened[-2:], "gx", 1)
    return jnp.concatenate([below, widened], axis=0)


def upper_sides_first(grads):
    widened = padded_2(grads, (("gy", 1), ("gz", 2)), 2)
    above = from_behind(widened[:2], "gx", -1)
    return jnp.concatenate([widened, above], axis=0)


def local(features, scales, occupancy, kernel, gamma, beta):
    size_x, size_y, size_z, channels = features.shape
    extent = (size_x, size_y, size_z)
    voxels = size_x * size_y * size_z
    feats = features.astype(jnp.float32).reshape(voxels, channels)
    occupied = expand_blocks(occupancy, OB)
    energy = beta[None, :] + jnp.dot(
        feats * feats, gamma, precision=lax.Precision.HIGHEST, preferred_element_type=jnp.float32
    )
    inv_root = lax.rsqrt(energy)
    latent = (occupied * feats * inv_root).astype(jnp.bfloat16)
    latent_grid = latent.reshape(size_x, size_y, size_z, channels)
    padded = lower_sides_first(latent_grid)
    mean = context_mean(padded, kernel, extent)
    latent_f = latent.astype(jnp.float32)
    scale_f = scales.astype(jnp.float32).reshape(voxels, channels)
    inverse = 1.0 / (scale_f * scale_f)
    mean_grad = (occupied * (mean - latent_f) * inverse).astype(jnp.bfloat16)
    grad_grid = mean_grad.reshape(size_x, size_y, size_z, channels)
    grad_pad = upper_sides_first(grad_grid)
    context_grad = context_transposed(grad_pad, kernel, extent)
    latent_grad = occupied * (context_grad + (latent_f - mean) * inverse)
    weighted = latent_grad * feats * inv_root * inv_root * inv_root
    coupled = jnp.dot(
        weighted, gamma.T, precision=lax.Precision.HIGHEST, preferred_element_type=jnp.float32
    )
    grad_features = (
        (latent_grad * inv_root - feats * coupled)
        .astype(jnp.bfloat16)
        .reshape(size_x, size_y, size_z, channels)
    )
    kernel_local = kernel_terms(padded, mean_grad, extent) / voxels
    grad_kernel = lax.psum_scatter(
        kernel_local, ("gx", "gy", "gz"), scatter_dimension=0, tiled=True
    )
    factor = 0.5 / math.sqrt(voxels)
    gamma_local = -factor * jnp.dot(
        (feats * feats).T,
        weighted,
        precision=lax.Precision.HIGHEST,
        preferred_element_type=jnp.float32,
    )
    beta_local = -factor * jnp.sum(weighted, axis=0)
    grad_gamma, grad_beta = lax.psum((gamma_local, beta_local), ("gx", "gy", "gz"))
    return (grad_features, grad_kernel, grad_gamma, grad_beta)


HIGHEST = lax.Precision.HIGHEST
F32 = jnp.float32
BF16 = jnp.bfloat16
EDGE = 8


def exchanged(value, axes, target):
    names = (axes,) if isinstance(axes, str) else axes
    sizes = [lax.axis_size(name) for name in names]
    places = [()]
    for size in sizes:
        places = [place + (i,) for place in places for i in range(size)]
    pairs = []
    for number, place in enumerate(places):
        goal = target(*place)
        if all(0 <= spot < size for spot, size in zip(goal, sizes)):
            flat = 0
            for spot, size in zip(goal, sizes):
                flat = flat * size + spot
            pairs.append((number, flat))
    return lax.ppermute(value, names if len(names) > 1 else names[0], pairs)


def flipped(value, axis):
    return exchanged(value, axis, lambda i: (1 - i,))


def occupied_rows(occupancy, extent, channels):
    size_x, size_y, size_z = extent
    level = lax.broadcasted_iota(jnp.int32, (size_z, channels), 0) // OB
    layers = []
    for bx in range(size_x // OB):
        lines = []
        for by in range(size_y // OB):
            column = jnp.zeros((size_z, channels), F32)
            for bz in range(size_z // OB):
                value = occupancy[bx, by, bz].astype(F32)
                column = jnp.where(level == bz, value, column)
            lines.append(jnp.broadcast_to(column[None, None], (OB, OB, size_z, channels)))
        layers.append(jnp.concatenate(lines, axis=1) if len(lines) > 1 else lines[0])
    mask = jnp.concatenate(layers, axis=0) if len(layers) > 1 else layers[0]
    return mask.reshape(size_x * size_y * size_z, channels)


def latent_kernel(
    far_features, far_scales, far_occupancy, far_gamma, far_beta,
    latent, across_y, first_x, second_x, root, features, gamma,
    scales, beta, occupancy, arrivals,
):
    loads = [
        pltpu.make_async_copy(far, near, arrivals.at[n])
        for n, (far, near) in enumerate(
            (
                (far_features, features),
                (far_gamma, gamma),
                (far_beta, beta),
                (far_occupancy, occupancy),
                (far_scales, scales),
            )
        )
    ]
    for load in loads:
        load.start()
    for load in loads:
        load.wait()
    size_x, _, _, channels = features.shape
    feats = features[...].astype(F32).reshape(-1, channels)
    energy = beta[...] + jnp.dot(
        feats * feats, gamma[...], precision=HIGHEST, preferred_element_type=F32
    )
    inv_root = lax.rsqrt(energy)
    root[...] = inv_root
    occupied = occupied_rows(occupancy, features.shape[:3], channels)
    rounded = (occupied * feats * inv_root).astype(BF16).reshape(features.shape)
    latent[...] = rounded
    scale = scales[...].astype(F32).reshape(-1, channels)
    signed = jnp.where(occupied > 0.0, scale, -scale).astype(BF16).reshape(features.shape)
    across_y[:size_x] = rounded
    across_y[size_x:] = signed
    upward = rounded[size_x - 2 :]
    downward = rounded[:2]
    odd = lax.rem(lax.axis_index("gx"), 2) == 1
    first_x[:2] = jnp.where(odd, downward, upward)
    second_x[:2] = jnp.where(odd, upward, downward)
    first_x[2:] = signed[:2]
    second_x[2:] = signed[:2]


def below_and_above(first, second):
    odd = lax.rem(lax.axis_index("gx"), 2) == 1
    return jnp.where(odd, first, second), jnp.where(odd, second, first)


def z_edges(wide, spot, across, size_z):
    first_z = lax.axis_index("gz") == 0
    across = across.astype(F32)
    wide[spot + (pl.ds(0, EDGE),)] = jnp.where(first_z, 0.0, across[:, :, size_z - EDGE :])
    wide[spot + (pl.ds(EDGE + size_z, EDGE),)] = jnp.where(first_z, across[:, :, :EDGE], 0.0)


def mean_kernel(
    own, side, first, corner, second, corner_2,
    own_z, side_z, first_z, corner_z, second_z, corner_2z,
    far_kernel, grad, rest, kernel, wide, shifted, level, held, arrival,
):
    load = pltpu.make_async_copy(far_kernel, kernel, arrival)
    load.start()
    size_x, _, size_z, channels = rest.shape
    size_y = own.shape[1]
    gy = lax.axis_index("gy")
    near_y, far_y = gy * size_y, (1 - gy) * size_y
    for at_y, block, block_z, one, two, one_z, two_z in (
        (near_y, own, own_z, first, second, first_z, second_z),
        (far_y, side, side_z, corner, corner_2, corner_z, corner_2z),
    ):
        spot_y = pl.ds(2 + at_y, size_y)
        below, above = below_and_above(one[...], two[...])
        below_z, above_z = below_and_above(one_z[...], two_z[...])
        for at_x, main, across in (
            (2, block[:size_x], block_z[:size_x]),
            (0, below[:2], below_z[:2]),
            (2 + size_x, above[:2], above_z[:2]),
        ):
            spot = (pl.ds(at_x, main.shape[0]), spot_y)
            wide[spot + (pl.ds(EDGE, size_z),)] = main.astype(F32)
            z_edges(wide, spot, across, size_z)
        level[:size_x, pl.ds(at_y, size_y)] = block[size_x:].astype(F32)
        level[size_x:, pl.ds(at_y, size_y)] = above[2:].astype(F32)
    blank = jnp.zeros((size_x + 4, 2) + wide.shape[2:], F32)
    wide[:, :2] = blank
    wide[:, 2 + 2 * size_y :] = blank
    for number in range(5):
        start = EDGE + number - 2
        shifted[:, :, :, number * channels : (number + 1) * channels] = wide[
            :, :, start : start + size_z, :
        ].astype(BF16)
    box = (size_x + 2, 2 * size_y, size_z, channels)
    load.wait()
    total = jnp.zeros((box[0] * box[1] * box[2], channels), F32)
    for along_x, along_y, _, count, first_tap in tap_groups():
        patch = shifted[
            2 + along_x : 2 + along_x + box[0],
            2 + along_y : 2 + along_y + box[1],
            :,
            : count * channels,
        ].reshape(-1, count * channels)
        weights = kernel[first_tap : first_tap + count].reshape(count * channels, channels)
        total = total + jnp.dot(patch, weights, preferred_element_type=F32)
    signed = level[...]
    latent = wide[2:, 2 : 2 + box[1], EDGE : EDGE + size_z]
    difference = (total.reshape(box) - latent) * (1.0 / (signed * signed))
    grad[...] = jnp.where(signed > 0.0, difference, 0.0).astype(BF16)
    held[...] = -difference[:size_x]
    rest[...] = held[:, pl.ds(near_y, size_y)]


def share_kernel(spanned, voxels, *refs):
    (own, side, first, corner, second, corner_2,
     own_z, side_z, first_z, corner_z, second_z, corner_2z, grad, grad_z) = refs[:14]
    mine, later, message, wide, flat, turned, product = refs[14:]
    rows = mine.shape[0]
    size_x, all_y, all_z, channels = flat.shape
    size_y, size_z = all_y // 2, all_z // 2
    gx, gy, gz = lax.axis_index("gx"), lax.axis_index("gy"), lax.axis_index("gz")
    blank = jnp.zeros((size_x + 2, 2, wide.shape[2], channels), F32)
    wide[:, :2] = blank
    wide[:, 2 + all_y :] = blank
    for start in (0, EDGE + all_z):
        wide[:, 2 : 2 + all_y, start : start + EDGE] = jnp.zeros((size_x + 2, all_y, EDGE, channels), F32)
    for here_y, here_z, block, one, two in (
        (True, True, own, first, second),
        (False, True, side, corner, corner_2),
        (True, False, own_z, first_z, second_z),
        (False, False, side_z, corner_z, corner_2z),
    ):
        at_y = (gy if here_y else 1 - gy) * size_y
        at_z = (gz if here_z else 1 - gz) * size_z
        spot_y, spot_z = pl.ds(2 + at_y, size_y), pl.ds(pl.multiple_of(EDGE + at_z, EDGE), size_z)
        wide[2:, spot_y, spot_z] = block[:size_x].astype(F32)
        wide[:2, spot_y, spot_z] = below_and_above(one[:2], two[:2])[0].astype(F32)
    flat[:, :, pl.ds(pl.multiple_of(gz * size_z, size_z), size_z)] = grad[:size_x]
    flat[:, :, pl.ds(pl.multiple_of((1 - gz) * size_z, size_z), size_z)] = grad_z[:size_x]
    turned[...] = flat[...].reshape(-1, channels).T
    for other in range(4):
        first_row = (((gx ^ other) * 2 + gy) * 2 + gz) * rows
        first_tap = jnp.minimum(first_row // channels, 62 - spanned)
        for level in range(5):
            number = lax.rem(level + 5 - lax.rem(first_tap, 5), 5)
            group = (first_tap + number) // 5
            along_x, along_y = group // 5, lax.rem(group, 5)
            start = EDGE + level - 2
            patch = wide[pl.ds(along_x, size_x), pl.ds(along_y, all_y), start : start + all_z]
            result = jnp.dot(
                turned[...], patch.astype(BF16).reshape(-1, channels), preferred_element_type=F32
            )
            product[other, pl.ds(pl.multiple_of(number * channels, channels), channels)] = result.T
        offset = pl.multiple_of(first_row - first_tap * channels, 16)
        share = product[other, pl.ds(offset, rows)] * (1.0 / voxels)
        if other == 0:
            mine[...] = share
        elif other == 2:
            later[...] = share
        else:
            half = (other // 2) * rows
            message[half : half + rows] = share.astype(message.dtype)


def feature_kernel(
    grad, grad_z, kernel, rest, root, features, gamma, block,
    grad_features, sums, wide, shifted,
):
    size_x, size_y, size_z, channels = features.shape
    voxels = size_x * size_y * size_z
    gy = lax.axis_index("gy")
    spot = (pl.ds(0, size_x + 2), pl.ds(2, 2 * size_y))
    wide[spot + (pl.ds(EDGE, size_z),)] = grad[...].astype(F32)
    z_edges(wide, spot, grad_z[...], size_z)
    blank = jnp.zeros((size_x + 2, 2) + wide.shape[2:], F32)
    wide[:, :2] = blank
    wide[:, 2 + 2 * size_y :] = blank
    for number in range(5):
        start = EDGE - (number - 2)
        shifted[:, :, :, number * channels : (number + 1) * channels] = wide[
            :, pl.ds(gy * size_y, size_y + 4), start : start + size_z, :
        ].astype(BF16)
    total = jnp.zeros((voxels, channels), F32)
    for along_x, along_y, _, count, first_tap in tap_groups():
        patch = shifted[
            -along_x : -along_x + size_x,
            2 - along_y : 2 - along_y + size_y,
            :,
            : count * channels,
        ].reshape(-1, count * channels)
        weights = jnp.concatenate([kernel[first_tap + k] for k in range(count)], axis=1)
        total = total + lax.dot_general(
            patch, weights, (((1,), (1,)), ((), ())), preferred_element_type=F32
        )
    occupied = jnp.where(block[size_x:].astype(F32).reshape(voxels, channels) > 0.0, 1.0, 0.0)
    latent_grad = occupied * (total + rest[...].reshape(voxels, channels))
    inv_root = root[...]
    feats = features[...].astype(F32).reshape(voxels, channels)
    weighted = latent_grad * feats * inv_root * inv_root * inv_root
    coupled = lax.dot_general(
        weighted, gamma[...], (((1,), (1,)), ((), ())), precision=HIGHEST, preferred_element_type=F32
    )
    grad_features[...] = (latent_grad * inv_root - feats * coupled).astype(BF16).reshape(features.shape)
    factor = 0.5 / math.sqrt(voxels)
    sums[:channels] = -factor * jnp.dot(
        (feats * feats).T, weighted, precision=HIGHEST, preferred_element_type=F32
    )
    ones = jnp.sum(weighted, axis=0, keepdims=True)
    sums[channels:] = -factor * jnp.broadcast_to(ones, (8, channels))


def call(body, outs, scratch, args, far=()):
    spaces = [pltpu.HBM if n in far else pltpu.VMEM for n in range(len(args))]
    args = [pltpu.with_memory_space_constraint(a, space) for a, space in zip(args, spaces)]
    return pl.pallas_call(
        body,
        out_shape=outs,
        in_specs=[pl.BlockSpec(memory_space=space) for space in spaces],
        out_specs=[pl.BlockSpec(memory_space=pltpu.VMEM)] * len(outs),
        scratch_shapes=scratch,
        compiler_params=pltpu.CompilerParams(vmem_limit_bytes=24 << 20),
    )(*args)


def fast_local(features, scales, occupancy, kernel, gamma, beta):
    shape = features.shape
    size_x, size_y, size_z, channels = shape
    voxels = size_x * size_y * size_z
    rest_of = shape[1:]
    latent, across_y, first_x, second_x, root, kept_features, kept_gamma = call(
        latent_kernel,
        [
            pltpu.VMEM(shape, BF16),
            pltpu.VMEM((2 * size_x,) + rest_of, BF16),
            pltpu.VMEM((4,) + rest_of, BF16),
            pltpu.VMEM((4,) + rest_of, BF16),
            pltpu.VMEM((voxels, channels), F32),
            pltpu.VMEM(shape, BF16),
            pltpu.VMEM(gamma.shape, F32),
        ],
        [
            pltpu.VMEM(shape, BF16),
            pltpu.VMEM((1, channels), F32),
            pltpu.SMEM(occupancy.shape, jnp.int32),
            pltpu.SemaphoreType.DMA((5,)),
        ],
        (features, scales, occupancy, gamma, beta.reshape(1, channels)),
        (0, 1, 2, 3, 4),
    )
    middle = lambda x: (3 - x if x in (1, 2) else -1,)
    side = flipped(across_y, "gy")
    first = exchanged(first_x, "gx", lambda x: (x ^ 1,))
    second = exchanged(second_x, "gx", middle)
    upward, downward = side[size_x - 2 : size_x], side[:2]
    odd = lax.rem(lax.axis_index("gx"), 2) == 1
    levels = side[size_x : size_x + 2]
    corner = exchanged(
        jnp.concatenate([jnp.where(odd, downward, upward), levels]), "gx", lambda x: (x ^ 1,)
    )
    corner_2 = exchanged(
        jnp.concatenate([jnp.where(odd, upward, downward), levels]), "gx", middle
    )
    sent = (side, first, corner, second, corner_2)
    around = (across_y,) + sent + tuple(flipped(part, "gz") for part in (latent,) + sent)
    wide_y = 2 * size_y + 4
    wide_z = size_z + 2 * EDGE
    grad, rest, kept_kernel = call(
        mean_kernel,
        [
            pltpu.VMEM((size_x + 2, 2 * size_y, size_z, channels), BF16),
            pltpu.VMEM(shape, F32),
            pltpu.VMEM(kernel.shape, BF16),
        ],
        [
            pltpu.VMEM((size_x + 4, wide_y, wide_z, channels), F32),
            pltpu.VMEM((size_x + 4, wide_y, size_z, 5 * channels), BF16),
            pltpu.VMEM((size_x + 2, 2 * size_y, size_z, channels), F32),
            pltpu.VMEM((size_x, 2 * size_y, size_z, channels), F32),
            pltpu.SemaphoreType.DMA,
        ],
        around + (kernel,),
        (12,),
    )
    grad_z = flipped(grad, "gz")
    rows = 62 * channels // 16
    spanned = 5
    mine, later, message = call(
        functools.partial(share_kernel, spanned, voxels),
        [pltpu.VMEM((rows, channels), F32)] * 2 + [pltpu.VMEM((2 * rows, channels), BF16)],
        [
            pltpu.VMEM((size_x + 2, wide_y, 2 * size_z + 2 * EDGE, channels), F32),
            pltpu.VMEM((size_x, 2 * size_y, 2 * size_z, channels), BF16),
            pltpu.VMEM((channels, 4 * voxels), BF16),
            pltpu.VMEM((4, spanned * channels, channels), F32),
        ],
        around + (grad, grad_z),
    )
    halves = exchanged(message, "gx", lambda x: (x ^ 1,))
    grad_features, sums = call(
        feature_kernel,
        [jax.ShapeDtypeStruct(shape, BF16), pltpu.VMEM((channels + 8, channels), F32)],
        [
            pltpu.VMEM((size_x + 2, wide_y, wide_z, channels), F32),
            pltpu.VMEM((size_x + 2, size_y + 4, size_z, 5 * channels), BF16),
        ],
        (grad, grad_z, kept_kernel, rest, root, kept_features, kept_gamma, across_y),
    )
    sums = sums + flipped(sums, "gz")
    quarter = exchanged((later + halves[rows:].astype(F32)).astype(BF16), "gx", lambda x: (x ^ 2,))
    sums = sums + flipped(sums, "gy")
    sums = sums + exchanged(sums, "gx", lambda x: (x ^ 1,))
    sums = sums + exchanged(sums, "gx", lambda x: (x ^ 2,))
    share = mine + halves[:rows].astype(F32) + quarter.astype(F32)
    return grad_features, share.reshape(-1), sums[:channels], sums[channels]


def chosen(features, scales, occupancy, kernel, gamma, beta):
    sizes = tuple(lax.axis_size(axis) for axis in ("gx", "gy", "gz"))
    size_x, size_y, size_z, channels = features.shape
    small = size_x >= 2 and size_y >= 2 and size_z % 16 == 0 and size_x * size_y * size_z <= 1024
    if sizes == (4, 2, 2) and small and channels == 128:
        return fast_local(features, scales, occupancy, kernel, gamma, beta)
    return local(features, scales, occupancy, kernel, gamma, beta)


def solution(mesh):
    return jax.shard_map(
        chosen,
        mesh=mesh,
        in_specs=(
            P(("groups", "gx"), "gy", "gz", None),
            P(("groups", "gx"), "gy", "gz", None),
            P(("groups", "gx"), "gy", "gz"),
            P(),
            P(),
            P(),
        ),
        out_specs=(
            P(("groups", "gx"), "gy", "gz", None),
            P(("groups", "gx", "gy", "gz")),
            P("groups", None),
            P("groups"),
        ),
        check_vma=False,
    )
```

```python
import functools
import math

import jax
import jax.numpy as jnp
from jax import lax
from jax.experimental import pallas as pl
from jax.experimental.pallas import tpu as pltpu
from jax.sharding import PartitionSpec as P

OB = 4


def padded_2(shard, sides, width):
    for axis, dim in sides:
        size, length = (lax.axis_size(axis), shard.shape[dim])
        up = [(i, (i + 1) % size) for i in range(size - 1)]
        down = [(j, i) for i, j in up]
        last = lax.slice_in_dim(shard, length - width, length, axis=dim)
        leading = lax.slice_in_dim(shard, 0, width, axis=dim)
        before = lax.ppermute(last, axis, up)
        after = lax.ppermute(leading, axis, down)
        shard = jnp.concatenate([before, shard, after], axis=dim)
    return shard


def from_behind(value, axis, steps):
    count = lax.axis_size(axis)
    leading, last = (max(0, -steps), min(count, count - steps))
    return lax.ppermute(value, axis, [(source, source + steps) for source in range(leading, last)])


def causal_offsets():
    result = []
    for along_x in range(-2, 3):
        for along_y in range(-2, 3):
            for along_z in range(-2, 3):
                if (along_x, along_y, along_z) < (0, 0, 0):
                    result.append((along_x, along_y, along_z))
    return result


def tap_groups():
    groups = []
    for number, offset in enumerate(causal_offsets()):
        if groups and groups[-1][0] == offset[0] and (groups[-1][1] == offset[1]):
            groups[-1][3] += 1
        else:
            groups.append([offset[0], offset[1], offset[2], 1, number])
    return groups


def expand_blocks(occupancy, edge):
    blocks_x, blocks_y, blocks_z = occupancy.shape
    grown = jnp.broadcast_to(
        occupancy[:, None, :, None, :, None], (blocks_x, edge, blocks_y, edge, blocks_z, edge)
    )
    return grown.reshape(-1, 1).astype(jnp.float32)


def forward_patch(padded, along_x, along_y, start_z, count, extent):
    size_x, size_y, size_z = extent
    pieces = [
        padded[
            2 + along_x : 2 + along_x + size_x,
            2 + along_y : 2 + along_y + size_y,
            2 + along_z : 2 + along_z + size_z,
        ]
        for along_z in range(start_z, start_z + count)
    ]
    return jnp.concatenate(pieces, axis=3).reshape(size_x * size_y * size_z, -1)


def context_mean(padded, kernel, extent):
    channels = kernel.shape[1]
    total = jnp.zeros((extent[0] * extent[1] * extent[2], channels), jnp.float32)
    for along_x, along_y, start_z, count, first_tap in tap_groups():
        patch = forward_patch(padded, along_x, along_y, start_z, count, extent)
        weights = kernel[first_tap : first_tap + count].reshape(count * channels, channels)
        total = total + jnp.dot(patch, weights, preferred_element_type=jnp.float32)
    return total


def context_transposed(padded, kernel, extent):
    size_x, size_y, size_z = extent
    channels = kernel.shape[1]
    total = jnp.zeros((size_x * size_y * size_z, channels), jnp.float32)
    for along_x, along_y, start_z, count, first_tap in tap_groups():
        pieces = [
            padded[
                -along_x : -along_x + size_x,
                2 - along_y : 2 - along_y + size_y,
                2 - along_z : 2 - along_z + size_z,
            ]
            for along_z in range(start_z, start_z + count)
        ]
        patch = jnp.concatenate(pieces, axis=3).reshape(size_x * size_y * size_z, -1)
        weights = jnp.transpose(kernel[first_tap : first_tap + count], (0, 2, 1)).reshape(
            count * channels, channels
        )
        total = total + jnp.dot(patch, weights, preferred_element_type=jnp.float32)
    return total


def kernel_terms(padded, mean_grad, extent):
    terms = []
    for along_x, along_y, start_z, count, first_tap in tap_groups():
        patch = forward_patch(padded, along_x, along_y, start_z, count, extent)
        terms.append(
            lax.dot_general(
                patch, mean_grad, (((0,), (0,)), ((), ())), preferred_element_type=jnp.float32
            )
        )
    return jnp.concatenate(terms, axis=0).reshape(-1)


def lower_sides_first(latent):
    widened = padded_2(latent, (("gy", 1), ("gz", 2)), 2)
    below = from_behind(widened[-2:], "gx", 1)
    return jnp.concatenate([below, widened], axis=0)


def upper_sides_first(grads):
    widened = padded_2(grads, (("gy", 1), ("gz", 2)), 2)
    above = from_behind(widened[:2], "gx", -1)
    return jnp.concatenate([widened, above], axis=0)


def local(features, scales, occupancy, kernel, gamma, beta):
    size_x, size_y, size_z, channels = features.shape
    extent = (size_x, size_y, size_z)
    voxels = size_x * size_y * size_z
    feats = features.astype(jnp.float32).reshape(voxels, channels)
    occupied = expand_blocks(occupancy, OB)
    energy = beta[None, :] + jnp.dot(
        feats * feats, gamma, precision=lax.Precision.HIGHEST, preferred_element_type=jnp.float32
    )
    inv_root = lax.rsqrt(energy)
    latent = (occupied * feats * inv_root).astype(jnp.bfloat16)
    latent_grid = latent.reshape(size_x, size_y, size_z, channels)
    padded = lower_sides_first(latent_grid)
    mean = context_mean(padded, kernel, extent)
    latent_f = latent.astype(jnp.float32)
    scale_f = scales.astype(jnp.float32).reshape(voxels, channels)
    inverse = 1.0 / (scale_f * scale_f)
    mean_grad = (occupied * (mean - latent_f) * inverse).astype(jnp.bfloat16)
    grad_grid = mean_grad.reshape(size_x, size_y, size_z, channels)
    grad_pad = upper_sides_first(grad_grid)
    context_grad = context_transposed(grad_pad, kernel, extent)
    latent_grad = occupied * (context_grad + (latent_f - mean) * inverse)
    weighted = latent_grad * feats * inv_root * inv_root * inv_root
    coupled = jnp.dot(
        weighted, gamma.T, precision=lax.Precision.HIGHEST, preferred_element_type=jnp.float32
    )
    grad_features = (
        (latent_grad * inv_root - feats * coupled)
        .astype(jnp.bfloat16)
        .reshape(size_x, size_y, size_z, channels)
    )
    kernel_local = kernel_terms(padded, mean_grad, extent) / voxels
    grad_kernel = lax.psum_scatter(
        kernel_local, ("gx", "gy", "gz"), scatter_dimension=0, tiled=True
    )
    factor = 0.5 / math.sqrt(voxels)
    gamma_local = -factor * jnp.dot(
        (feats * feats).T,
        weighted,
        precision=lax.Precision.HIGHEST,
        preferred_element_type=jnp.float32,
    )
    beta_local = -factor * jnp.sum(weighted, axis=0)
    grad_gamma, grad_beta = lax.psum((gamma_local, beta_local), ("gx", "gy", "gz"))
    return (grad_features, grad_kernel, grad_gamma, grad_beta)


HIGHEST = lax.Precision.HIGHEST
F32 = jnp.float32
BF16 = jnp.bfloat16
EDGE = 8


def exchanged(value, axes, target):
    names = (axes,) if isinstance(axes, str) else axes
    sizes = [lax.axis_size(name) for name in names]
    places = [()]
    for size in sizes:
        places = [place + (i,) for place in places for i in range(size)]
    pairs = []
    for number, place in enumerate(places):
        goal = target(*place)
        if all(0 <= spot < size for spot, size in zip(goal, sizes)):
            flat = 0
            for spot, size in zip(goal, sizes):
                flat = flat * size + spot
            pairs.append((number, flat))
    return lax.ppermute(value, names if len(names) > 1 else names[0], pairs)


def flipped(value, axis):
    return exchanged(value, axis, lambda i: (1 - i,))


def occupied_rows(occupancy, extent, channels):
    size_x, size_y, size_z = extent
    level = lax.broadcasted_iota(jnp.int32, (size_z, channels), 0) // OB
    layers = []
    for bx in range(size_x // OB):
        lines = []
        for by in range(size_y // OB):
            column = jnp.zeros((size_z, channels), F32)
            for bz in range(size_z // OB):
                value = occupancy[bx, by, bz].astype(F32)
                column = jnp.where(level == bz, value, column)
            lines.append(jnp.broadcast_to(column[None, None], (OB, OB, size_z, channels)))
        layers.append(jnp.concatenate(lines, axis=1) if len(lines) > 1 else lines[0])
    mask = jnp.concatenate(layers, axis=0) if len(layers) > 1 else layers[0]
    return mask.reshape(size_x * size_y * size_z, channels)


def latent_kernel(
    far_features, far_scales, far_occupancy, far_gamma, far_beta,
    latent, across_y, first_x, second_x, root, features, gamma,
    scales, beta, occupancy, arrivals,
):
    loads = [
        pltpu.make_async_copy(far, near, arrivals.at[n])
        for n, (far, near) in enumerate(
            (
                (far_features, features),
                (far_gamma, gamma),
                (far_beta, beta),
                (far_occupancy, occupancy),
                (far_scales, scales),
            )
        )
    ]
    for load in loads:
        load.start()
    for load in loads:
        load.wait()
    size_x, _, _, channels = features.shape
    feats = features[...].astype(F32).reshape(-1, channels)
    energy = beta[...] + jnp.dot(
        feats * feats, gamma[...], precision=HIGHEST, preferred_element_type=F32
    )
    inv_root = lax.rsqrt(energy)
    root[...] = inv_root
    occupied = occupied_rows(occupancy, features.shape[:3], channels)
    rounded = (occupied * feats * inv_root).astype(BF16).reshape(features.shape)
    latent[...] = rounded
    scale = scales[...].astype(F32).reshape(-1, channels)
    signed = jnp.where(occupied > 0.0, scale, -scale).astype(BF16).reshape(features.shape)
    across_y[:size_x] = rounded
    across_y[size_x:] = signed
    upward = rounded[size_x - 2 :]
    downward = rounded[:2]
    odd = lax.rem(lax.axis_index("gx"), 2) == 1
    first_x[:2] = jnp.where(odd, downward, upward)
    second_x[:2] = jnp.where(odd, upward, downward)
    first_x[2:] = signed[:2]
    second_x[2:] = signed[:2]


def below_and_above(first, second):
    gx = lax.axis_index("gx")
    odd = lax.rem(gx, 2) == 1
    second = jnp.where(jnp.logical_or(gx == 1, gx == 2), second, jnp.zeros_like(second))
    return jnp.where(odd, first, second), jnp.where(odd, second, first)


def z_edges(wide, spot, across, size_z):
    first_z = lax.axis_index("gz") == 0
    across = across.astype(F32)
    wide[spot + (pl.ds(0, EDGE),)] = jnp.where(first_z, 0.0, across[:, :, size_z - EDGE :])
    wide[spot + (pl.ds(EDGE + size_z, EDGE),)] = jnp.where(first_z, across[:, :, :EDGE], 0.0)


def mean_kernel(
    own, side, first, corner, second, corner_2,
    own_z, side_z, first_z, corner_z, second_z, corner_2z,
    far_kernel, grad, rest, kernel, wide, shifted, level, held, arrival,
):
    load = pltpu.make_async_copy(far_kernel, kernel, arrival)
    load.start()
    size_x, _, size_z, channels = rest.shape
    size_y = own.shape[1]
    gy = lax.axis_index("gy")
    near_y, far_y = gy * size_y, (1 - gy) * size_y
    for at_y, block, block_z, one, two, one_z, two_z in (
        (near_y, own, own_z, first, second, first_z, second_z),
        (far_y, side, side_z, corner, corner_2, corner_z, corner_2z),
    ):
        spot_y = pl.ds(2 + at_y, size_y)
        below, above = below_and_above(one[...], two[...])
        below_z, above_z = below_and_above(one_z[...], two_z[...])
        for at_x, main, across in (
            (2, block[:size_x], block_z[:size_x]),
            (0, below[:2], below_z[:2]),
            (2 + size_x, above[:2], above_z[:2]),
        ):
            spot = (pl.ds(at_x, main.shape[0]), spot_y)
            wide[spot + (pl.ds(EDGE, size_z),)] = main.astype(F32)
            z_edges(wide, spot, across, size_z)
        level[:size_x, pl.ds(at_y, size_y)] = block[size_x:].astype(F32)
        level[size_x:, pl.ds(at_y, size_y)] = above[2:].astype(F32)
    blank = jnp.zeros((size_x + 4, 2) + wide.shape[2:], F32)
    wide[:, :2] = blank
    wide[:, 2 + 2 * size_y :] = blank
    for number in range(5):
        start = EDGE + number - 2
        shifted[:, :, :, number * channels : (number + 1) * channels] = wide[
            :, :, start : start + size_z, :
        ].astype(BF16)
    box = (size_x + 2, 2 * size_y, size_z, channels)
    load.wait()
    def product(first_x, layers, first_y, lines, taps, count):
        patch = shifted[
            first_x : first_x + layers, first_y : first_y + lines, :, : count * channels
        ].reshape(-1, count * channels)
        columns = [kernel[tap : tap + count].reshape(count * channels, channels) for tap in taps]
        weights = jnp.concatenate(columns, axis=1) if len(columns) > 1 else columns[0]
        out = jnp.dot(patch, weights, preferred_element_type=F32)
        return out.reshape(layers, lines, size_z, len(taps) * channels)

    total = jnp.zeros(box, F32)
    for along_y in range(5):
        pair = product(0, box[0] + 1, along_y, box[1], (5 * along_y, 25 + 5 * along_y), 5)
        total = total + pair[:-1, :, :, :channels] + pair[1:, :, :, channels:]
    pair = product(2, box[0], 0, box[1] + 1, (50, 55), 5)
    total = total + pair[:, :-1, :, :channels] + pair[:, 1:, :, channels:]
    total = total + product(2, box[0], 2, box[1], (60,), 2)
    signed = level[...]
    latent = wide[2:, 2 : 2 + box[1], EDGE : EDGE + size_z]
    difference = (total - latent) * (1.0 / (signed * signed))
    grad[...] = jnp.where(signed > 0.0, difference, 0.0).astype(BF16)
    held[...] = -difference[:size_x]
    rest[...] = held[:, pl.ds(near_y, size_y)]


def share_kernel(spanned, voxels, *refs):
    (own, side, first, corner, second, corner_2,
     own_z, side_z, first_z, corner_z, second_z, corner_2z, grad, grad_z) = refs[:14]
    mine, later, message, wide, flat, turned, product = refs[14:]
    rows = mine.shape[0]
    size_x, all_y, all_z, channels = flat.shape
    size_y, size_z = all_y // 2, all_z // 2
    gx, gy, gz = lax.axis_index("gx"), lax.axis_index("gy"), lax.axis_index("gz")
    blank = jnp.zeros((size_x + 2, 2, wide.shape[2], channels), F32)
    wide[:, :2] = blank
    wide[:, 2 + all_y :] = blank
    for start in (0, EDGE + all_z):
        wide[:, 2 : 2 + all_y, start : start + EDGE] = jnp.zeros((size_x + 2, all_y, EDGE, channels), F32)
    for here_y, here_z, block, one, two in (
        (True, True, own, first, second),
        (False, True, side, corner, corner_2),
        (True, False, own_z, first_z, second_z),
        (False, False, side_z, corner_z, corner_2z),
    ):
        at_y = (gy if here_y else 1 - gy) * size_y
        at_z = (gz if here_z else 1 - gz) * size_z
        spot_y, spot_z = pl.ds(2 + at_y, size_y), pl.ds(pl.multiple_of(EDGE + at_z, EDGE), size_z)
        wide[2:, spot_y, spot_z] = block[:size_x].astype(F32)
        wide[:2, spot_y, spot_z] = below_and_above(one[:2], two[:2])[0].astype(F32)
    flat[:, :, pl.ds(pl.multiple_of(gz * size_z, size_z), size_z)] = grad[:size_x]
    flat[:, :, pl.ds(pl.multiple_of((1 - gz) * size_z, size_z), size_z)] = grad_z[:size_x]
    turned[...] = flat[...].reshape(-1, channels).T
    for other in range(4):
        first_row = (((gx ^ other) * 2 + gy) * 2 + gz) * rows
        first_tap = jnp.minimum(first_row // channels, 62 - spanned)
        for level in range(5):
            number = lax.rem(level + 5 - lax.rem(first_tap, 5), 5)
            group = (first_tap + number) // 5
            along_x, along_y = group // 5, lax.rem(group, 5)
            start = EDGE + level - 2
            patch = wide[pl.ds(along_x, size_x), pl.ds(along_y, all_y), start : start + all_z]
            result = jnp.dot(
                turned[...], patch.astype(BF16).reshape(-1, channels), preferred_element_type=F32
            )
            product[other, pl.ds(pl.multiple_of(number * channels, channels), channels)] = result.T
        offset = pl.multiple_of(first_row - first_tap * channels, 16)
        share = product[other, pl.ds(offset, rows)] * (1.0 / voxels)
        if other == 0:
            mine[...] = share
        elif other == 3:
            later[...] = share
        else:
            half = (other - 1) * rows
            message[half : half + rows] = share.astype(message.dtype)


def feature_kernel(
    grad, grad_z, kernel, rest, root, features, gamma, block,
    grad_features, mine, theirs, wide, shifted,
):
    size_x, size_y, size_z, channels = features.shape
    voxels = size_x * size_y * size_z
    gy = lax.axis_index("gy")
    spot = (pl.ds(0, size_x + 2), pl.ds(2, 2 * size_y))
    wide[spot + (pl.ds(EDGE, size_z),)] = grad[...].astype(F32)
    z_edges(wide, spot, grad_z[...], size_z)
    blank = jnp.zeros((size_x + 2, 2) + wide.shape[2:], F32)
    wide[:, :2] = blank
    wide[:, 2 + 2 * size_y :] = blank
    for number in range(5):
        start = EDGE - (number - 2)
        shifted[:, :, :, number * channels : (number + 1) * channels] = wide[
            :, pl.ds(gy * size_y, size_y + 4), start : start + size_z, :
        ].astype(BF16)
    total = jnp.zeros((voxels, channels), F32)
    for along_x, along_y, _, count, first_tap in tap_groups():
        patch = shifted[
            -along_x : -along_x + size_x,
            2 - along_y : 2 - along_y + size_y,
            :,
            : count * channels,
        ].reshape(-1, count * channels)
        weights = jnp.concatenate([kernel[first_tap + k] for k in range(count)], axis=1)
        total = total + lax.dot_general(
            patch, weights, (((1,), (1,)), ((), ())), preferred_element_type=F32
        )
    occupied = jnp.where(block[size_x:].astype(F32).reshape(voxels, channels) > 0.0, 1.0, 0.0)
    latent_grad = occupied * (total + rest[...].reshape(voxels, channels))
    inv_root = root[...]
    feats = features[...].astype(F32).reshape(voxels, channels)
    weighted = latent_grad * feats * inv_root * inv_root * inv_root
    coupled = lax.dot_general(
        weighted, gamma[...], (((1,), (1,)), ((), ())), precision=HIGHEST, preferred_element_type=F32
    )
    grad_features[...] = (latent_grad * inv_root - feats * coupled).astype(BF16).reshape(features.shape)
    factor = 0.5 / math.sqrt(voxels)
    sums = -factor * jnp.dot(
        (feats * feats).T, weighted, precision=HIGHEST, preferred_element_type=F32
    )
    ones = -factor * jnp.broadcast_to(jnp.sum(weighted, axis=0, keepdims=True), (8, channels))
    half = channels // 2
    first_z = lax.axis_index("gz") == 0
    mine[:half] = jnp.where(first_z, sums[:half], sums[half:])
    theirs[:half] = jnp.where(first_z, sums[half:], sums[:half])
    mine[half:] = ones
    theirs[half:] = ones


def join_kernel(mine, theirs, kept, halves, quarter, gamma, beta, share):
    rows = share.shape[0]
    share[...] = kept[...] + halves[:rows].astype(F32) + quarter[...].astype(F32)
    half = gamma.shape[0] // 2
    first_z = lax.axis_index("gz") == 0
    own, other = mine[:half], theirs[:half]
    gamma[:half] = jnp.where(first_z, own, other)
    gamma[half:] = jnp.where(first_z, other, own)
    beta[...] = mine[half : half + 1]


def call(body, outs, scratch, args, far=()):
    spaces = [pltpu.HBM if n in far else pltpu.VMEM for n in range(len(args))]
    args = [pltpu.with_memory_space_constraint(a, space) for a, space in zip(args, spaces)]
    return pl.pallas_call(
        body,
        out_shape=outs,
        in_specs=[pl.BlockSpec(memory_space=space) for space in spaces],
        out_specs=[pl.BlockSpec(memory_space=pltpu.VMEM)] * len(outs),
        scratch_shapes=scratch,
        compiler_params=pltpu.CompilerParams(vmem_limit_bytes=24 << 20),
    )(*args)


def fast_local(features, scales, occupancy, kernel, gamma, beta):
    shape = features.shape
    size_x, size_y, size_z, channels = shape
    voxels = size_x * size_y * size_z
    rest_of = shape[1:]
    latent, across_y, first_x, second_x, root, kept_features, kept_gamma = call(
        latent_kernel,
        [
            pltpu.VMEM(shape, BF16),
            pltpu.VMEM((2 * size_x,) + rest_of, BF16),
            pltpu.VMEM((4,) + rest_of, BF16),
            pltpu.VMEM((4,) + rest_of, BF16),
            pltpu.VMEM((voxels, channels), F32),
            pltpu.VMEM(shape, BF16),
            pltpu.VMEM(gamma.shape, F32),
        ],
        [
            pltpu.VMEM(shape, BF16),
            pltpu.VMEM((1, channels), F32),
            pltpu.SMEM(occupancy.shape, jnp.int32),
            pltpu.SemaphoreType.DMA((5,)),
        ],
        (features, scales, occupancy, gamma, beta.reshape(1, channels)),
        (0, 1, 2, 3, 4),
    )
    middle = lambda x, z: (3 - x, z) if x in (1, 2) else (x, 1 - z)
    side = flipped(across_y, "gy")
    first = exchanged(first_x, "gx", lambda x: (x ^ 1,))
    second = exchanged(second_x, ("gx", "gz"), middle)
    corner = exchanged(first_x, ("gx", "gy"), lambda x, y: (x ^ 1, 1 - y))
    corner_2 = exchanged(
        second_x, ("gx", "gy", "gz"), lambda x, y, z: (3 - x, 1 - y, z) if x in (1, 2) else (x, y, 1 - z)
    )
    sent = (side, first, corner, second, corner_2)
    around = (across_y,) + sent + tuple(flipped(part, "gz") for part in (latent,) + sent)
    wide_y = 2 * size_y + 4
    wide_z = size_z + 2 * EDGE
    grad, rest, kept_kernel = call(
        mean_kernel,
        [
            pltpu.VMEM((size_x + 2, 2 * size_y, size_z, channels), BF16),
            pltpu.VMEM(shape, F32),
            pltpu.VMEM(kernel.shape, BF16),
        ],
        [
            pltpu.VMEM((size_x + 4, wide_y, wide_z, channels), F32),
            pltpu.VMEM((size_x + 4, wide_y, size_z, 5 * channels), BF16),
            pltpu.VMEM((size_x + 2, 2 * size_y, size_z, channels), F32),
            pltpu.VMEM((size_x, 2 * size_y, size_z, channels), F32),
            pltpu.SemaphoreType.DMA,
        ],
        around + (kernel,),
        (12,),
    )
    grad_z = flipped(grad, "gz")
    rows = 62 * channels // 16
    spanned = 5
    mine, later, message = call(
        functools.partial(share_kernel, spanned, voxels),
        [pltpu.VMEM((rows, channels), F32)] * 2 + [pltpu.VMEM((2 * rows, channels), BF16)],
        [
            pltpu.VMEM((size_x + 2, wide_y, 2 * size_z + 2 * EDGE, channels), F32),
            pltpu.VMEM((size_x, 2 * size_y, 2 * size_z, channels), BF16),
            pltpu.VMEM((channels, 4 * voxels), BF16),
            pltpu.VMEM((4, spanned * channels, channels), F32),
        ],
        around + (grad, grad_z),
    )
    halves = exchanged(message, "gx", lambda x: (x ^ 1,))
    grad_features, sums, others = call(
        feature_kernel,
        [jax.ShapeDtypeStruct(shape, BF16)] + [pltpu.VMEM((channels // 2 + 8, channels), F32)] * 2,
        [
            pltpu.VMEM((size_x + 2, wide_y, wide_z, channels), F32),
            pltpu.VMEM((size_x + 2, size_y + 4, size_z, 5 * channels), BF16),
        ],
        (grad, grad_z, kept_kernel, rest, root, kept_features, kept_gamma, across_y),
    )
    sums = sums + flipped(others, "gz")
    quarter = exchanged((later + halves[rows:].astype(F32)).astype(BF16), "gx", lambda x: (3 - x,))
    sums = sums + flipped(sums, "gy")
    sums = sums + exchanged(sums, "gx", lambda x: (x ^ 1,))
    sums = sums + exchanged(sums, "gx", lambda x: (x ^ 2,))
    struct = jax.ShapeDtypeStruct
    grad_gamma, grad_beta, share = call(
        join_kernel,
        [struct((channels, channels), F32), struct((1, channels), F32), struct((rows, channels), F32)],
        [],
        (sums, flipped(sums, "gz"), mine, halves, quarter),
    )
    return grad_features, share.reshape(-1), grad_gamma, grad_beta.reshape(channels)


def chosen(features, scales, occupancy, kernel, gamma, beta):
    sizes = tuple(lax.axis_size(axis) for axis in ("gx", "gy", "gz"))
    size_x, size_y, size_z, channels = features.shape
    small = size_x >= 2 and size_y >= 2 and size_z % 16 == 0 and size_x * size_y * size_z <= 1024
    if sizes == (4, 2, 2) and small and channels == 128:
        return fast_local(features, scales, occupancy, kernel, gamma, beta)
    return local(features, scales, occupancy, kernel, gamma, beta)


def solution(mesh):
    return jax.shard_map(
        chosen,
        mesh=mesh,
        in_specs=(
            P(("groups", "gx"), "gy", "gz", None),
            P(("groups", "gx"), "gy", "gz", None),
            P(("groups", "gx"), "gy", "gz"),
            P(),
            P(),
            P(),
        ),
        out_specs=(
            P(("groups", "gx"), "gy", "gz", None),
            P(("groups", "gx", "gy", "gz")),
            P("groups", None),
            P("groups"),
        ),
        check_vma=False,
    )
```

```python
import functools
import math

import jax
import jax.numpy as jnp
from jax import lax
from jax.experimental import pallas as pl
from jax.experimental.pallas import tpu as pltpu
from jax.sharding import PartitionSpec as P

OB = 4


def padded_2(shard, sides, width):
    for axis, dim in sides:
        size, length = (lax.axis_size(axis), shard.shape[dim])
        up = [(i, (i + 1) % size) for i in range(size - 1)]
        down = [(j, i) for i, j in up]
        last = lax.slice_in_dim(shard, length - width, length, axis=dim)
        leading = lax.slice_in_dim(shard, 0, width, axis=dim)
        before = lax.ppermute(last, axis, up)
        after = lax.ppermute(leading, axis, down)
        shard = jnp.concatenate([before, shard, after], axis=dim)
    return shard


def from_behind(value, axis, steps):
    count = lax.axis_size(axis)
    leading, last = (max(0, -steps), min(count, count - steps))
    return lax.ppermute(value, axis, [(source, source + steps) for source in range(leading, last)])


def causal_offsets():
    result = []
    for along_x in range(-2, 3):
        for along_y in range(-2, 3):
            for along_z in range(-2, 3):
                if (along_x, along_y, along_z) < (0, 0, 0):
                    result.append((along_x, along_y, along_z))
    return result


def tap_groups():
    groups = []
    for number, offset in enumerate(causal_offsets()):
        if groups and groups[-1][0] == offset[0] and (groups[-1][1] == offset[1]):
            groups[-1][3] += 1
        else:
            groups.append([offset[0], offset[1], offset[2], 1, number])
    return groups


def expand_blocks(occupancy, edge):
    blocks_x, blocks_y, blocks_z = occupancy.shape
    grown = jnp.broadcast_to(
        occupancy[:, None, :, None, :, None], (blocks_x, edge, blocks_y, edge, blocks_z, edge)
    )
    return grown.reshape(-1, 1).astype(jnp.float32)


def forward_patch(padded, along_x, along_y, start_z, count, extent):
    size_x, size_y, size_z = extent
    pieces = [
        padded[
            2 + along_x : 2 + along_x + size_x,
            2 + along_y : 2 + along_y + size_y,
            2 + along_z : 2 + along_z + size_z,
        ]
        for along_z in range(start_z, start_z + count)
    ]
    return jnp.concatenate(pieces, axis=3).reshape(size_x * size_y * size_z, -1)


def context_mean(padded, kernel, extent):
    channels = kernel.shape[1]
    total = jnp.zeros((extent[0] * extent[1] * extent[2], channels), jnp.float32)
    for along_x, along_y, start_z, count, first_tap in tap_groups():
        patch = forward_patch(padded, along_x, along_y, start_z, count, extent)
        weights = kernel[first_tap : first_tap + count].reshape(count * channels, channels)
        total = total + jnp.dot(patch, weights, preferred_element_type=jnp.float32)
    return total


def context_transposed(padded, kernel, extent):
    size_x, size_y, size_z = extent
    channels = kernel.shape[1]
    total = jnp.zeros((size_x * size_y * size_z, channels), jnp.float32)
    for along_x, along_y, start_z, count, first_tap in tap_groups():
        pieces = [
            padded[
                -along_x : -along_x + size_x,
                2 - along_y : 2 - along_y + size_y,
                2 - along_z : 2 - along_z + size_z,
            ]
            for along_z in range(start_z, start_z + count)
        ]
        patch = jnp.concatenate(pieces, axis=3).reshape(size_x * size_y * size_z, -1)
        weights = jnp.transpose(kernel[first_tap : first_tap + count], (0, 2, 1)).reshape(
            count * channels, channels
        )
        total = total + jnp.dot(patch, weights, preferred_element_type=jnp.float32)
    return total


def kernel_terms(padded, mean_grad, extent):
    terms = []
    for along_x, along_y, start_z, count, first_tap in tap_groups():
        patch = forward_patch(padded, along_x, along_y, start_z, count, extent)
        terms.append(
            lax.dot_general(
                patch, mean_grad, (((0,), (0,)), ((), ())), preferred_element_type=jnp.float32
            )
        )
    return jnp.concatenate(terms, axis=0).reshape(-1)


def lower_sides_first(latent):
    widened = padded_2(latent, (("gy", 1), ("gz", 2)), 2)
    below = from_behind(widened[-2:], "gx", 1)
    return jnp.concatenate([below, widened], axis=0)


def upper_sides_first(grads):
    widened = padded_2(grads, (("gy", 1), ("gz", 2)), 2)
    above = from_behind(widened[:2], "gx", -1)
    return jnp.concatenate([widened, above], axis=0)


def local(features, scales, occupancy, kernel, gamma, beta):
    size_x, size_y, size_z, channels = features.shape
    extent = (size_x, size_y, size_z)
    voxels = size_x * size_y * size_z
    feats = features.astype(jnp.float32).reshape(voxels, channels)
    occupied = expand_blocks(occupancy, OB)
    energy = beta[None, :] + jnp.dot(
        feats * feats, gamma, precision=lax.Precision.HIGHEST, preferred_element_type=jnp.float32
    )
    inv_root = lax.rsqrt(energy)
    latent = (occupied * feats * inv_root).astype(jnp.bfloat16)
    latent_grid = latent.reshape(size_x, size_y, size_z, channels)
    padded = lower_sides_first(latent_grid)
    mean = context_mean(padded, kernel, extent)
    latent_f = latent.astype(jnp.float32)
    scale_f = scales.astype(jnp.float32).reshape(voxels, channels)
    inverse = 1.0 / (scale_f * scale_f)
    mean_grad = (occupied * (mean - latent_f) * inverse).astype(jnp.bfloat16)
    grad_grid = mean_grad.reshape(size_x, size_y, size_z, channels)
    grad_pad = upper_sides_first(grad_grid)
    context_grad = context_transposed(grad_pad, kernel, extent)
    latent_grad = occupied * (context_grad + (latent_f - mean) * inverse)
    weighted = latent_grad * feats * inv_root * inv_root * inv_root
    coupled = jnp.dot(
        weighted, gamma.T, precision=lax.Precision.HIGHEST, preferred_element_type=jnp.float32
    )
    grad_features = (
        (latent_grad * inv_root - feats * coupled)
        .astype(jnp.bfloat16)
        .reshape(size_x, size_y, size_z, channels)
    )
    kernel_local = kernel_terms(padded, mean_grad, extent) / voxels
    grad_kernel = lax.psum_scatter(
        kernel_local, ("gx", "gy", "gz"), scatter_dimension=0, tiled=True
    )
    factor = 0.5 / math.sqrt(voxels)
    gamma_local = -factor * jnp.dot(
        (feats * feats).T,
        weighted,
        precision=lax.Precision.HIGHEST,
        preferred_element_type=jnp.float32,
    )
    beta_local = -factor * jnp.sum(weighted, axis=0)
    grad_gamma, grad_beta = lax.psum((gamma_local, beta_local), ("gx", "gy", "gz"))
    return (grad_features, grad_kernel, grad_gamma, grad_beta)


HIGHEST = lax.Precision.HIGHEST
F32 = jnp.float32
BF16 = jnp.bfloat16
EDGE = 8


def exchanged(value, axes, target):
    names = (axes,) if isinstance(axes, str) else axes
    sizes = [lax.axis_size(name) for name in names]
    places = [()]
    for size in sizes:
        places = [place + (i,) for place in places for i in range(size)]
    pairs = []
    for number, place in enumerate(places):
        goal = target(*place)
        if all(0 <= spot < size for spot, size in zip(goal, sizes)):
            flat = 0
            for spot, size in zip(goal, sizes):
                flat = flat * size + spot
            pairs.append((number, flat))
    return lax.ppermute(value, names if len(names) > 1 else names[0], pairs)


def flipped(value, axis):
    return exchanged(value, axis, lambda i: (1 - i,))


def occupied_rows(occupancy, extent, channels):
    size_x, size_y, size_z = extent
    level = lax.broadcasted_iota(jnp.int32, (size_z, channels), 0) // OB
    layers = []
    for bx in range(size_x // OB):
        lines = []
        for by in range(size_y // OB):
            column = jnp.zeros((size_z, channels), F32)
            for bz in range(size_z // OB):
                value = occupancy[bx, by, bz].astype(F32)
                column = jnp.where(level == bz, value, column)
            lines.append(jnp.broadcast_to(column[None, None], (OB, OB, size_z, channels)))
        layers.append(jnp.concatenate(lines, axis=1) if len(lines) > 1 else lines[0])
    mask = jnp.concatenate(layers, axis=0) if len(layers) > 1 else layers[0]
    return mask.reshape(size_x * size_y * size_z, channels)


def latent_kernel(
    far_features, far_scales, far_occupancy, far_gamma, far_beta,
    latent, across_y, first_x, second_x, root, features, gamma,
    scales, beta, occupancy, arrivals,
):
    loads = [
        pltpu.make_async_copy(far, near, arrivals.at[n])
        for n, (far, near) in enumerate(
            (
                (far_features, features),
                (far_gamma, gamma),
                (far_beta, beta),
                (far_occupancy, occupancy),
                (far_scales, scales),
            )
        )
    ]
    for load in loads:
        load.start()
    for load in loads:
        load.wait()
    size_x, _, _, channels = features.shape
    feats = features[...].astype(F32).reshape(-1, channels)
    energy = beta[...] + jnp.dot(
        feats * feats, gamma[...], precision=HIGHEST, preferred_element_type=F32
    )
    inv_root = lax.rsqrt(energy)
    root[...] = inv_root
    occupied = occupied_rows(occupancy, features.shape[:3], channels)
    rounded = (occupied * feats * inv_root).astype(BF16).reshape(features.shape)
    latent[...] = rounded
    scale = scales[...].astype(F32).reshape(-1, channels)
    signed = jnp.where(occupied > 0.0, scale, -scale).astype(BF16).reshape(features.shape)
    across_y[:size_x] = rounded
    across_y[size_x:] = signed
    upward = rounded[size_x - 2 :]
    downward = rounded[:2]
    odd = lax.rem(lax.axis_index("gx"), 2) == 1
    first_x[:2] = jnp.where(odd, downward, upward)
    second_x[:2] = jnp.where(odd, upward, downward)
    first_x[2:] = signed[:2]
    second_x[2:] = signed[:2]


def below_and_above(first, second):
    gx = lax.axis_index("gx")
    odd = lax.rem(gx, 2) == 1
    second = jnp.where(jnp.logical_or(gx == 1, gx == 2), second, jnp.zeros_like(second))
    return jnp.where(odd, first, second), jnp.where(odd, second, first)


def z_edges(wide, spot, across, size_z, low=0):
    first_z = lax.axis_index("gz") == low
    across = across.astype(F32)
    wide[spot + (pl.ds(0, EDGE),)] = jnp.where(first_z, 0.0, across[:, :, size_z - EDGE :])
    wide[spot + (pl.ds(EDGE + size_z, EDGE),)] = jnp.where(first_z, across[:, :, :EDGE], 0.0)


def load_kernel(far, near, arrival):
    taps = far.shape[0]
    cuts = [n * taps // 4 for n in range(5)]
    loads = [
        pltpu.make_async_copy(far.at[low:high], near.at[low:high], arrival.at[n])
        for n, (low, high) in enumerate(zip(cuts[:-1], cuts[1:]))
    ]
    for load in loads:
        load.start()
    for load in loads:
        load.wait()


def mean_kernel(
    own, side, first, corner, second, corner_2,
    own_z, side_z, first_z, corner_z, second_z, corner_2z,
    kernel, grad, rest, wide, shifted, level, held,
):
    size_x, _, size_z, channels = rest.shape
    size_y = own.shape[1]
    gy = lax.axis_index("gy")
    near_y, far_y = gy * size_y, (1 - gy) * size_y
    for at_y, block, block_z, one, two, one_z, two_z in (
        (near_y, own, own_z, first, second, first_z, second_z),
        (far_y, side, side_z, corner, corner_2, corner_z, corner_2z),
    ):
        spot_y = pl.ds(2 + at_y, size_y)
        below, above = below_and_above(one[...], two[...])
        below_z, above_z = below_and_above(one_z[...], two_z[...])
        for at_x, main, across in (
            (2, block[:size_x], block_z[:size_x]),
            (0, below[:2], below_z[:2]),
            (2 + size_x, above[:2], above_z[:2]),
        ):
            spot = (pl.ds(at_x, main.shape[0]), spot_y)
            wide[spot + (pl.ds(EDGE, size_z),)] = main.astype(F32)
            z_edges(wide, spot, across, size_z)
        level[:size_x, pl.ds(at_y, size_y)] = block[size_x:].astype(F32)
        level[size_x:, pl.ds(at_y, size_y)] = above[2:].astype(F32)
    blank = jnp.zeros((size_x + 4, 2) + wide.shape[2:], F32)
    wide[:, :2] = blank
    wide[:, 2 + 2 * size_y :] = blank
    for number in range(5):
        start = EDGE + number - 2
        shifted[:, :, :, number * channels : (number + 1) * channels] = wide[
            :, :, start : start + size_z, :
        ].astype(BF16)
    box = (size_x + 2, 2 * size_y, size_z, channels)

    def product(first_x, layers, first_y, lines, taps, count):
        patch = shifted[
            first_x : first_x + layers, first_y : first_y + lines, :, : count * channels
        ].reshape(-1, count * channels)
        columns = [kernel[tap : tap + count].reshape(count * channels, channels) for tap in taps]
        weights = jnp.concatenate(columns, axis=1) if len(columns) > 1 else columns[0]
        out = jnp.dot(patch, weights, preferred_element_type=F32)
        return out.reshape(layers, lines, size_z, len(taps) * channels)

    total = jnp.zeros(box, F32)
    for along_y in range(5):
        pair = product(0, box[0] + 1, along_y, box[1], (5 * along_y, 25 + 5 * along_y), 5)
        total = total + pair[:-1, :, :, :channels] + pair[1:, :, :, channels:]
    pair = product(2, box[0], 0, box[1] + 1, (50, 55), 5)
    total = total + pair[:, :-1, :, :channels] + pair[:, 1:, :, channels:]
    total = total + product(2, box[0], 2, box[1], (60,), 2)
    signed = level[...]
    latent = wide[2:, 2 : 2 + box[1], EDGE : EDGE + size_z]
    difference = (total - latent) * (1.0 / (signed * signed))
    grad[...] = jnp.where(signed > 0.0, difference, 0.0).astype(BF16)
    held[...] = -difference[:size_x]
    rest[...] = held[:, pl.ds(near_y, size_y)]


def share_taps(rows, channels, spanned):
    gx, gy, gz = lax.axis_index("gx"), lax.axis_index("gy"), lax.axis_index("gz")
    taps = []
    for other in range(4):
        first_row = (((gx ^ other) * 2 + gy) * 2 + gz) * rows
        first_tap = jnp.minimum(first_row // channels, 62 - spanned)
        taps.append((first_row - first_tap * channels, first_tap))
    return taps


def products(wide, turned, box, taps):
    size_x, all_y, size_z, channels = box
    for level in range(5):
        start = EDGE + level - 2
        for pair in ((0, 1), (2, 3)):
            patches, spots = [], []
            for other in pair:
                first_tap = taps[other][1]
                number = lax.rem(level + 5 - lax.rem(first_tap, 5), 5)
                group = (first_tap + number) // 5
                patch = wide[
                    pl.ds(group // 5, size_x), pl.ds(lax.rem(group, 5), all_y), start : start + size_z
                ]
                patches.append(patch.astype(BF16).reshape(-1, channels))
                spots.append(pl.ds(pl.multiple_of(number * channels, channels), channels))
            result = jnp.dot(
                turned[...], jnp.concatenate(patches, axis=1), preferred_element_type=F32
            )
            for n, other in enumerate(pair):
                yield other, spots[n], result[:, n * channels : (n + 1) * channels]


def partial_kernel(spanned, rows, *refs):
    (own, side, first, corner, second, corner_2,
     own_z, side_z, first_z, corner_z, second_z, corner_2z, grad, wide) = refs[:14]
    partial, across, turned = refs[14:]
    size_x, _, size_z, channels = own_z.shape
    all_y = grad.shape[1]
    size_y = all_y // 2
    gy = lax.axis_index("gy")
    for at_y, block, block_z, one, two, one_z, two_z in (
        (gy * size_y, own, own_z, first, second, first_z, second_z),
        ((1 - gy) * size_y, side, side_z, corner, corner_2, corner_z, corner_2z),
    ):
        below = below_and_above(one[:2], two[:2])[0]
        below_z = below_and_above(one_z[:2], two_z[:2])[0]
        for at_x, main, edge in (
            (2, block_z[:size_x], block[:size_x]),
            (0, below_z, below),
        ):
            spot = (pl.ds(at_x, main.shape[0]), pl.ds(2 + at_y, size_y))
            across[spot + (pl.ds(EDGE, size_z),)] = main.astype(F32)
            z_edges(across, spot, edge, size_z, 1)
    blank = jnp.zeros((size_x + 2, 2) + across.shape[2:], F32)
    across[:, :2] = blank
    across[:, 2 + all_y :] = blank
    turned[...] = grad[:size_x].reshape(-1, channels).T
    box = (size_x, all_y, size_z, channels)
    for other, spot, value in products(wide, turned, box, share_taps(rows, channels, spanned)):
        partial[other, spot] = value


def share_kernel(spanned, voxels, partial, across, grad_z, mine, later, message, turned, product):
    rows, channels = mine.shape
    size_x = across.shape[0] - 2
    all_y, size_z = grad_z.shape[1:3]
    turned[...] = grad_z[:size_x].reshape(-1, channels).T
    taps = share_taps(rows, channels, spanned)
    for other, spot, value in products(across, turned, (size_x, all_y, size_z, channels), taps):
        product[other, spot] = (partial[other, spot] + value).T
    for other in range(4):
        offset = pl.multiple_of(taps[other][0], 16)
        share = product[other, pl.ds(offset, rows)] * (1.0 / voxels)
        if other == 0:
            mine[...] = share
        elif other == 3:
            later[...] = share
        else:
            half = (other - 1) * rows
            message[half : half + rows] = share.astype(message.dtype)


def feature_kernel(
    grad, grad_z, kernel, rest, root, features, gamma, block,
    grad_features, mine, theirs, wide, shifted,
):
    size_x, size_y, size_z, channels = features.shape
    voxels = size_x * size_y * size_z
    gy = lax.axis_index("gy")
    spot = (pl.ds(0, size_x + 2), pl.ds(2, 2 * size_y))
    wide[spot + (pl.ds(EDGE, size_z),)] = grad[...].astype(F32)
    z_edges(wide, spot, grad_z[...], size_z)
    blank = jnp.zeros((size_x + 2, 2) + wide.shape[2:], F32)
    wide[:, :2] = blank
    wide[:, 2 + 2 * size_y :] = blank
    for number in range(5):
        start = EDGE - (number - 2)
        shifted[:, :, :, number * channels : (number + 1) * channels] = wide[
            :, pl.ds(gy * size_y, size_y + 4), start : start + size_z, :
        ].astype(BF16)

    def transposed(first_x, layers, first_y, lines, taps, count):
        patch = shifted[
            first_x : first_x + layers, first_y : first_y + lines, :, : count * channels
        ].reshape(-1, count * channels)
        rows = [jnp.concatenate([kernel[tap + k] for k in range(count)], axis=1) for tap in taps]
        weights = jnp.concatenate(rows, axis=0) if len(rows) > 1 else rows[0]
        out = lax.dot_general(
            patch, weights, (((1,), (1,)), ((), ())), preferred_element_type=F32
        )
        return out.reshape(layers, lines, size_z, len(taps) * channels)

    total = jnp.zeros((size_x, size_y, size_z, channels), F32)
    for along_y in range(5):
        pair = transposed(1, size_x + 1, 4 - along_y, size_y, (5 * along_y, 25 + 5 * along_y), 5)
        total = total + pair[1:, :, :, :channels] + pair[:-1, :, :, channels:]
    pair = transposed(0, size_x, 3, size_y + 1, (50, 55), 5)
    total = total + pair[:, 1:, :, :channels] + pair[:, :-1, :, channels:]
    total = total + transposed(0, size_x, 2, size_y, (60,), 2)
    total = total.reshape(voxels, channels)
    occupied = jnp.where(block[size_x:].astype(F32).reshape(voxels, channels) > 0.0, 1.0, 0.0)
    latent_grad = occupied * (total + rest[...].reshape(voxels, channels))
    inv_root = root[...]
    feats = features[...].astype(F32).reshape(voxels, channels)
    weighted = latent_grad * feats * inv_root * inv_root * inv_root
    coupled = lax.dot_general(
        weighted, gamma[...], (((1,), (1,)), ((), ())), precision=HIGHEST, preferred_element_type=F32
    )
    grad_features[...] = (latent_grad * inv_root - feats * coupled).astype(BF16).reshape(features.shape)
    factor = 0.5 / math.sqrt(voxels)
    sums = -factor * jnp.dot(
        (feats * feats).T, weighted, precision=HIGHEST, preferred_element_type=F32
    )
    ones = -factor * jnp.broadcast_to(jnp.sum(weighted, axis=0, keepdims=True), (8, channels))
    half = channels // 2
    first_z = lax.axis_index("gz") == 0
    mine[:half] = jnp.where(first_z, sums[:half], sums[half:])
    theirs[:half] = jnp.where(first_z, sums[half:], sums[:half])
    mine[half:] = ones
    theirs[half:] = ones


def join_kernel(mine, theirs, kept, halves, quarter, gamma, beta, share):
    rows = share.shape[0]
    share[...] = kept[...] + halves[:rows].astype(F32) + quarter[...].astype(F32)
    half = gamma.shape[0] // 2
    first_z = lax.axis_index("gz") == 0
    own, other = mine[:half], theirs[:half]
    gamma[:half] = jnp.where(first_z, own, other)
    gamma[half:] = jnp.where(first_z, other, own)
    beta[...] = mine[half : half + 1]


def call(body, outs, scratch, args, far=()):
    spaces = [pltpu.HBM if n in far else pltpu.VMEM for n in range(len(args))]
    args = [pltpu.with_memory_space_constraint(a, space) for a, space in zip(args, spaces)]
    return pl.pallas_call(
        body,
        out_shape=outs,
        in_specs=[pl.BlockSpec(memory_space=space) for space in spaces],
        out_specs=[pl.BlockSpec(memory_space=pltpu.VMEM)] * len(outs),
        scratch_shapes=scratch,
        compiler_params=pltpu.CompilerParams(vmem_limit_bytes=24 << 20),
    )(*args)


def fast_local(features, scales, occupancy, kernel, gamma, beta):
    shape = features.shape
    size_x, size_y, size_z, channels = shape
    voxels = size_x * size_y * size_z
    rest_of = shape[1:]
    latent, across_y, first_x, second_x, root, kept_features, kept_gamma = call(
        latent_kernel,
        [
            pltpu.VMEM(shape, BF16),
            pltpu.VMEM((2 * size_x,) + rest_of, BF16),
            pltpu.VMEM((4,) + rest_of, BF16),
            pltpu.VMEM((4,) + rest_of, BF16),
            pltpu.VMEM((voxels, channels), F32),
            pltpu.VMEM(shape, BF16),
            pltpu.VMEM(gamma.shape, F32),
        ],
        [
            pltpu.VMEM(shape, BF16),
            pltpu.VMEM((1, channels), F32),
            pltpu.SMEM(occupancy.shape, jnp.int32),
            pltpu.SemaphoreType.DMA((5,)),
        ],
        (features, scales, occupancy, gamma, beta.reshape(1, channels)),
        (0, 1, 2, 3, 4),
    )
    middle = lambda x, z: (3 - x, z) if x in (1, 2) else (x, 1 - z)
    side = flipped(across_y, "gy")
    corner = exchanged(first_x, ("gx", "gy"), lambda x, y: (x ^ 1, 1 - y))
    first = exchanged(first_x, "gx", lambda x: (x ^ 1,))
    corner_2 = exchanged(
        second_x, ("gx", "gy", "gz"), lambda x, y, z: (3 - x, 1 - y, z) if x in (1, 2) else (x, y, 1 - z)
    )
    second = exchanged(second_x, ("gx", "gz"), middle)
    sent = (side, first, corner, second, corner_2)
    around = (across_y,) + sent + tuple(flipped(part, "gz") for part in (latent,) + sent)
    wide_y = 2 * size_y + 4
    wide_z = size_z + 2 * EDGE
    kept_kernel, = call(
        load_kernel, [pltpu.VMEM(kernel.shape, BF16)], [pltpu.SemaphoreType.DMA((4,))], (kernel,), (0,)
    )
    grad, rest, wide = call(
        mean_kernel,
        [
            pltpu.VMEM((size_x + 2, 2 * size_y, size_z, channels), BF16),
            pltpu.VMEM(shape, F32),
            pltpu.VMEM((size_x + 4, wide_y, wide_z, channels), F32),
        ],
        [
            pltpu.VMEM((size_x + 4, wide_y, size_z, 5 * channels), BF16),
            pltpu.VMEM((size_x + 2, 2 * size_y, size_z, channels), F32),
            pltpu.VMEM((size_x, 2 * size_y, size_z, channels), F32),
        ],
        around + (kept_kernel,),
    )
    grad_z = flipped(grad, "gz")
    rows = 62 * channels // 16
    spanned = 5
    turned = pltpu.VMEM((channels, 2 * voxels), BF16)
    pieces = (4, spanned * channels, channels)
    partial, across = call(
        functools.partial(partial_kernel, spanned, rows),
        [pltpu.VMEM(pieces, F32), pltpu.VMEM((size_x + 2, wide_y, wide_z, channels), F32)],
        [turned],
        around + (grad, wide),
    )
    mine, later, message = call(
        functools.partial(share_kernel, spanned, voxels),
        [pltpu.VMEM((rows, channels), F32)] * 2 + [pltpu.VMEM((2 * rows, channels), BF16)],
        [turned, pltpu.VMEM(pieces, F32)],
        (partial, across, grad_z),
    )
    halves = exchanged(message, "gx", lambda x: (x ^ 1,))
    grad_features, sums, others = call(
        feature_kernel,
        [jax.ShapeDtypeStruct(shape, BF16)] + [pltpu.VMEM((channels // 2 + 8, channels), F32)] * 2,
        [
            pltpu.VMEM((size_x + 2, wide_y, wide_z, channels), F32),
            pltpu.VMEM((size_x + 2, size_y + 4, size_z, 5 * channels), BF16),
        ],
        (grad, grad_z, kept_kernel, rest, root, kept_features, kept_gamma, across_y),
    )
    sums = sums + flipped(others, "gz")
    quarter = exchanged((later + halves[rows:].astype(F32)).astype(BF16), "gx", lambda x: (3 - x,))
    sums = sums + flipped(sums, "gy")
    sums = sums + exchanged(sums, "gx", lambda x: (x ^ 1,))
    sums = sums + exchanged(sums, "gx", lambda x: (x ^ 2,))
    struct = jax.ShapeDtypeStruct
    grad_gamma, grad_beta, share = call(
        join_kernel,
        [struct((channels, channels), F32), struct((1, channels), F32), struct((rows, channels), F32)],
        [],
        (sums, flipped(sums, "gz"), mine, halves, quarter),
    )
    return grad_features, share.reshape(-1), grad_gamma, grad_beta.reshape(channels)


def chosen(features, scales, occupancy, kernel, gamma, beta):
    sizes = tuple(lax.axis_size(axis) for axis in ("gx", "gy", "gz"))
    size_x, size_y, size_z, channels = features.shape
    small = size_x >= 2 and size_y >= 2 and size_z % 16 == 0 and size_x * size_y * size_z <= 1024
    if sizes == (4, 2, 2) and small and channels == 128:
        return fast_local(features, scales, occupancy, kernel, gamma, beta)
    return local(features, scales, occupancy, kernel, gamma, beta)


def solution(mesh):
    step = jax.shard_map(
        chosen,
        mesh=mesh,
        in_specs=(
            P(("groups", "gx"), "gy", "gz", None),
            P(("groups", "gx"), "gy", "gz", None),
            P(("groups", "gx"), "gy", "gz"),
            P(),
            P(),
            P(),
        ),
        out_specs=(
            P(("groups", "gx"), "gy", "gz", None),
            P(("groups", "gx", "gy", "gz")),
            P("groups", None),
            P("groups"),
        ),
        check_vma=False,
    )
    if tuple(mesh.shape[axis] for axis in ("gx", "gy", "gz")) != (4, 2, 2):
        return step
    return step
```

```python
import functools
import math

import jax
import jax.numpy as jnp
from jax import lax
from jax.experimental import pallas as pl
from jax.experimental.pallas import tpu as pltpu
from jax.sharding import PartitionSpec as P

OB = 4


def padded_2(shard, sides, width):
    for axis, dim in sides:
        size, length = (lax.axis_size(axis), shard.shape[dim])
        up = [(i, (i + 1) % size) for i in range(size - 1)]
        down = [(j, i) for i, j in up]
        last = lax.slice_in_dim(shard, length - width, length, axis=dim)
        leading = lax.slice_in_dim(shard, 0, width, axis=dim)
        before = lax.ppermute(last, axis, up)
        after = lax.ppermute(leading, axis, down)
        shard = jnp.concatenate([before, shard, after], axis=dim)
    return shard


def from_behind(value, axis, steps):
    count = lax.axis_size(axis)
    leading, last = (max(0, -steps), min(count, count - steps))
    return lax.ppermute(value, axis, [(source, source + steps) for source in range(leading, last)])


def causal_offsets():
    result = []
    for along_x in range(-2, 3):
        for along_y in range(-2, 3):
            for along_z in range(-2, 3):
                if (along_x, along_y, along_z) < (0, 0, 0):
                    result.append((along_x, along_y, along_z))
    return result


def tap_groups():
    groups = []
    for number, offset in enumerate(causal_offsets()):
        if groups and groups[-1][0] == offset[0] and (groups[-1][1] == offset[1]):
            groups[-1][3] += 1
        else:
            groups.append([offset[0], offset[1], offset[2], 1, number])
    return groups


def expand_blocks(occupancy, edge):
    blocks_x, blocks_y, blocks_z = occupancy.shape
    grown = jnp.broadcast_to(
        occupancy[:, None, :, None, :, None], (blocks_x, edge, blocks_y, edge, blocks_z, edge)
    )
    return grown.reshape(-1, 1).astype(jnp.float32)


def forward_patch(padded, along_x, along_y, start_z, count, extent):
    size_x, size_y, size_z = extent
    pieces = [
        padded[
            2 + along_x : 2 + along_x + size_x,
            2 + along_y : 2 + along_y + size_y,
            2 + along_z : 2 + along_z + size_z,
        ]
        for along_z in range(start_z, start_z + count)
    ]
    return jnp.concatenate(pieces, axis=3).reshape(size_x * size_y * size_z, -1)


def context_mean(padded, kernel, extent):
    channels = kernel.shape[1]
    total = jnp.zeros((extent[0] * extent[1] * extent[2], channels), jnp.float32)
    for along_x, along_y, start_z, count, first_tap in tap_groups():
        patch = forward_patch(padded, along_x, along_y, start_z, count, extent)
        weights = kernel[first_tap : first_tap + count].reshape(count * channels, channels)
        total = total + jnp.dot(patch, weights, preferred_element_type=jnp.float32)
    return total


def context_transposed(padded, kernel, extent):
    size_x, size_y, size_z = extent
    channels = kernel.shape[1]
    total = jnp.zeros((size_x * size_y * size_z, channels), jnp.float32)
    for along_x, along_y, start_z, count, first_tap in tap_groups():
        pieces = [
            padded[
                -along_x : -along_x + size_x,
                2 - along_y : 2 - along_y + size_y,
                2 - along_z : 2 - along_z + size_z,
            ]
            for along_z in range(start_z, start_z + count)
        ]
        patch = jnp.concatenate(pieces, axis=3).reshape(size_x * size_y * size_z, -1)
        weights = jnp.transpose(kernel[first_tap : first_tap + count], (0, 2, 1)).reshape(
            count * channels, channels
        )
        total = total + jnp.dot(patch, weights, preferred_element_type=jnp.float32)
    return total


def kernel_terms(padded, mean_grad, extent):
    terms = []
    for along_x, along_y, start_z, count, first_tap in tap_groups():
        patch = forward_patch(padded, along_x, along_y, start_z, count, extent)
        terms.append(
            lax.dot_general(
                patch, mean_grad, (((0,), (0,)), ((), ())), preferred_element_type=jnp.float32
            )
        )
    return jnp.concatenate(terms, axis=0).reshape(-1)


def lower_sides_first(latent):
    widened = padded_2(latent, (("gy", 1), ("gz", 2)), 2)
    below = from_behind(widened[-2:], "gx", 1)
    return jnp.concatenate([below, widened], axis=0)


def upper_sides_first(grads):
    widened = padded_2(grads, (("gy", 1), ("gz", 2)), 2)
    above = from_behind(widened[:2], "gx", -1)
    return jnp.concatenate([widened, above], axis=0)


def local(features, scales, occupancy, kernel, gamma, beta):
    size_x, size_y, size_z, channels = features.shape
    extent = (size_x, size_y, size_z)
    voxels = size_x * size_y * size_z
    feats = features.astype(jnp.float32).reshape(voxels, channels)
    occupied = expand_blocks(occupancy, OB)
    energy = beta[None, :] + jnp.dot(
        feats * feats, gamma, precision=lax.Precision.HIGHEST, preferred_element_type=jnp.float32
    )
    inv_root = lax.rsqrt(energy)
    latent = (occupied * feats * inv_root).astype(jnp.bfloat16)
    latent_grid = latent.reshape(size_x, size_y, size_z, channels)
    padded = lower_sides_first(latent_grid)
    mean = context_mean(padded, kernel, extent)
    latent_f = latent.astype(jnp.float32)
    scale_f = scales.astype(jnp.float32).reshape(voxels, channels)
    inverse = 1.0 / (scale_f * scale_f)
    mean_grad = (occupied * (mean - latent_f) * inverse).astype(jnp.bfloat16)
    grad_grid = mean_grad.reshape(size_x, size_y, size_z, channels)
    grad_pad = upper_sides_first(grad_grid)
    context_grad = context_transposed(grad_pad, kernel, extent)
    latent_grad = occupied * (context_grad + (latent_f - mean) * inverse)
    weighted = latent_grad * feats * inv_root * inv_root * inv_root
    coupled = jnp.dot(
        weighted, gamma.T, precision=lax.Precision.HIGHEST, preferred_element_type=jnp.float32
    )
    grad_features = (
        (latent_grad * inv_root - feats * coupled)
        .astype(jnp.bfloat16)
        .reshape(size_x, size_y, size_z, channels)
    )
    kernel_local = kernel_terms(padded, mean_grad, extent) / voxels
    grad_kernel = lax.psum_scatter(
        kernel_local, ("gx", "gy", "gz"), scatter_dimension=0, tiled=True
    )
    factor = 0.5 / math.sqrt(voxels)
    gamma_local = -factor * jnp.dot(
        (feats * feats).T,
        weighted,
        precision=lax.Precision.HIGHEST,
        preferred_element_type=jnp.float32,
    )
    beta_local = -factor * jnp.sum(weighted, axis=0)
    grad_gamma, grad_beta = lax.psum((gamma_local, beta_local), ("gx", "gy", "gz"))
    return (grad_features, grad_kernel, grad_gamma, grad_beta)


HIGHEST = lax.Precision.HIGHEST
F32 = jnp.float32
BF16 = jnp.bfloat16
EDGE = 8


def exchanged(value, axes, target):
    names = (axes,) if isinstance(axes, str) else axes
    sizes = [lax.axis_size(name) for name in names]
    places = [()]
    for size in sizes:
        places = [place + (i,) for place in places for i in range(size)]
    pairs = []
    for number, place in enumerate(places):
        goal = target(*place)
        if all(0 <= spot < size for spot, size in zip(goal, sizes)):
            flat = 0
            for spot, size in zip(goal, sizes):
                flat = flat * size + spot
            pairs.append((number, flat))
    return lax.ppermute(value, names if len(names) > 1 else names[0], pairs)


def flipped(value, axis):
    return exchanged(value, axis, lambda i: (1 - i,))


def occupied_rows(occupancy, extent, channels):
    size_x, size_y, size_z = extent
    level = lax.broadcasted_iota(jnp.int32, (size_z, channels), 0) // OB
    layers = []
    for bx in range(size_x // OB):
        lines = []
        for by in range(size_y // OB):
            column = jnp.zeros((size_z, channels), F32)
            for bz in range(size_z // OB):
                value = occupancy[bx, by, bz].astype(F32)
                column = jnp.where(level == bz, value, column)
            lines.append(jnp.broadcast_to(column[None, None], (OB, OB, size_z, channels)))
        layers.append(jnp.concatenate(lines, axis=1) if len(lines) > 1 else lines[0])
    mask = jnp.concatenate(layers, axis=0) if len(layers) > 1 else layers[0]
    return mask.reshape(size_x * size_y * size_z, channels)


def latent_kernel(
    far_features, far_scales, far_occupancy, far_gamma, far_beta,
    latent, across_y, first_x, second_x, root, features, gamma,
    scales, beta, occupancy, arrivals,
):
    loads = [
        pltpu.make_async_copy(far, near, arrivals.at[n])
        for n, (far, near) in enumerate(
            (
                (far_features, features),
                (far_gamma, gamma),
                (far_beta, beta),
                (far_occupancy, occupancy),
                (far_scales, scales),
            )
        )
    ]
    for load in loads:
        load.start()
    for load in loads:
        load.wait()
    size_x, _, _, channels = features.shape
    feats = features[...].astype(F32).reshape(-1, channels)
    energy = beta[...] + jnp.dot(
        feats * feats, gamma[...], precision=HIGHEST, preferred_element_type=F32
    )
    inv_root = lax.rsqrt(energy)
    root[...] = inv_root
    occupied = occupied_rows(occupancy, features.shape[:3], channels)
    rounded = (occupied * feats * inv_root).astype(BF16).reshape(features.shape)
    latent[...] = rounded
    scale = scales[...].astype(F32).reshape(-1, channels)
    signed = jnp.where(occupied > 0.0, scale, -scale).astype(BF16).reshape(features.shape)
    across_y[:size_x] = rounded
    across_y[size_x:] = signed
    upward = rounded[size_x - 2 :]
    downward = rounded[:2]
    odd = lax.rem(lax.axis_index("gx"), 2) == 1
    first_x[:2] = jnp.where(odd, downward, upward)
    second_x[:2] = jnp.where(odd, upward, downward)
    first_x[2:] = signed[:2]
    second_x[2:] = signed[:2]


def below_and_above(first, second):
    gx = lax.axis_index("gx")
    odd = lax.rem(gx, 2) == 1
    second = jnp.where(jnp.logical_or(gx == 1, gx == 2), second, jnp.zeros_like(second))
    return jnp.where(odd, first, second), jnp.where(odd, second, first)


def z_edges(wide, spot, across, size_z, low=0):
    first_z = lax.axis_index("gz") == low
    across = across.astype(F32)
    wide[spot + (pl.ds(0, EDGE),)] = jnp.where(first_z, 0.0, across[:, :, size_z - EDGE :])
    wide[spot + (pl.ds(EDGE + size_z, EDGE),)] = jnp.where(first_z, across[:, :, :EDGE], 0.0)


def load_kernel(far, near, arrival):
    taps = far.shape[0]
    cuts = [n * taps // 4 for n in range(5)]
    loads = [
        pltpu.make_async_copy(far.at[low:high], near.at[low:high], arrival.at[n])
        for n, (low, high) in enumerate(zip(cuts[:-1], cuts[1:]))
    ]
    for load in loads:
        load.start()
    for load in loads:
        load.wait()


def mean_kernel(
    own, side, first, corner, second, corner_2,
    own_z, side_z, first_z, corner_z, second_z, corner_2z,
    kernel, grad, rest, wide, shifted, level, held,
):
    size_x, _, size_z, channels = rest.shape
    size_y = own.shape[1]
    gy = lax.axis_index("gy")
    near_y, far_y = gy * size_y, (1 - gy) * size_y
    for at_y, block, block_z, one, two, one_z, two_z in (
        (near_y, own, own_z, first, second, first_z, second_z),
        (far_y, side, side_z, corner, corner_2, corner_z, corner_2z),
    ):
        spot_y = pl.ds(2 + at_y, size_y)
        below, above = below_and_above(one[...], two[...])
        below_z, above_z = below_and_above(one_z[...], two_z[...])
        for at_x, main, across in (
            (2, block[:size_x], block_z[:size_x]),
            (0, below[:2], below_z[:2]),
            (2 + size_x, above[:2], above_z[:2]),
        ):
            spot = (pl.ds(at_x, main.shape[0]), spot_y)
            wide[spot + (pl.ds(EDGE, size_z),)] = main.astype(F32)
            z_edges(wide, spot, across, size_z)
        level[:size_x, pl.ds(at_y, size_y)] = block[size_x:].astype(F32)
        level[size_x:, pl.ds(at_y, size_y)] = above[2:].astype(F32)
    blank = jnp.zeros((size_x + 4, 2) + wide.shape[2:], F32)
    wide[:, :2] = blank
    wide[:, 2 + 2 * size_y :] = blank
    for number in range(5):
        start = EDGE + number - 2
        shifted[:, :, :, number * channels : (number + 1) * channels] = wide[
            :, :, start : start + size_z, :
        ].astype(BF16)
    box = (size_x + 2, 2 * size_y, size_z, channels)

    def product(first_x, layers, first_y, lines, taps, count):
        patch = shifted[
            first_x : first_x + layers, first_y : first_y + lines, :, : count * channels
        ].reshape(-1, count * channels)
        columns = [kernel[tap : tap + count].reshape(count * channels, channels) for tap in taps]
        weights = jnp.concatenate(columns, axis=1) if len(columns) > 1 else columns[0]
        out = jnp.dot(patch, weights, preferred_element_type=F32)
        return out.reshape(layers, lines, size_z, len(taps) * channels)

    total = jnp.zeros(box, F32)
    for along_y in range(5):
        pair = product(0, box[0] + 1, along_y, box[1], (5 * along_y, 25 + 5 * along_y), 5)
        total = total + pair[:-1, :, :, :channels] + pair[1:, :, :, channels:]
    pair = product(2, box[0], 0, box[1] + 1, (50, 55), 5)
    total = total + pair[:, :-1, :, :channels] + pair[:, 1:, :, channels:]
    total = total + product(2, box[0], 2, box[1], (60,), 2)
    signed = level[...]
    latent = wide[2:, 2 : 2 + box[1], EDGE : EDGE + size_z]
    difference = (total - latent) * (1.0 / (signed * signed))
    grad[...] = jnp.where(signed > 0.0, difference, 0.0).astype(BF16)
    held[...] = -difference[:size_x]
    rest[...] = held[:, pl.ds(near_y, size_y)]


def share_taps(rows, channels, spanned):
    gx, gy, gz = lax.axis_index("gx"), lax.axis_index("gy"), lax.axis_index("gz")
    taps = []
    for other in range(4):
        first_row = (((gx ^ other) * 2 + gy) * 2 + gz) * rows
        first_tap = jnp.minimum(first_row // channels, 62 - spanned)
        taps.append((first_row - first_tap * channels, first_tap))
    return taps


def products(wide, turned, box, taps):
    size_x, all_y, size_z, channels = box
    for level in range(5):
        start = EDGE + level - 2
        for pair in ((0, 1), (2, 3)):
            patches, spots = [], []
            for other in pair:
                first_tap = taps[other][1]
                number = lax.rem(level + 5 - lax.rem(first_tap, 5), 5)
                group = (first_tap + number) // 5
                patch = wide[
                    pl.ds(group // 5, size_x), pl.ds(lax.rem(group, 5), all_y), start : start + size_z
                ]
                patches.append(patch.astype(BF16).reshape(-1, channels))
                spots.append(pl.ds(pl.multiple_of(number * channels, channels), channels))
            result = jnp.dot(
                turned[...], jnp.concatenate(patches, axis=1), preferred_element_type=F32
            )
            for n, other in enumerate(pair):
                yield other, spots[n], result[:, n * channels : (n + 1) * channels]


def partial_kernel(spanned, rows, *refs):
    (own, side, first, corner, second, corner_2,
     own_z, side_z, first_z, corner_z, second_z, corner_2z, grad, wide) = refs[:14]
    partial, across, turned = refs[14:]
    size_x, _, size_z, channels = own_z.shape
    all_y = grad.shape[1]
    size_y = all_y // 2
    gy = lax.axis_index("gy")
    for at_y, block, block_z, one, two, one_z, two_z in (
        (gy * size_y, own, own_z, first, second, first_z, second_z),
        ((1 - gy) * size_y, side, side_z, corner, corner_2, corner_z, corner_2z),
    ):
        below = below_and_above(one[:2], two[:2])[0]
        below_z = below_and_above(one_z[:2], two_z[:2])[0]
        for at_x, main, edge in (
            (2, block_z[:size_x], block[:size_x]),
            (0, below_z, below),
        ):
            spot = (pl.ds(at_x, main.shape[0]), pl.ds(2 + at_y, size_y))
            across[spot + (pl.ds(EDGE, size_z),)] = main.astype(F32)
            z_edges(across, spot, edge, size_z, 1)
    blank = jnp.zeros((size_x + 2, 2) + across.shape[2:], F32)
    across[:, :2] = blank
    across[:, 2 + all_y :] = blank
    turned[...] = grad[:size_x].reshape(-1, channels).T
    box = (size_x, all_y, size_z, channels)
    for other, spot, value in products(wide, turned, box, share_taps(rows, channels, spanned)):
        partial[other, spot] = value


def share_kernel(spanned, voxels, partial, across, grad_z, mine, later, ahead, direct, turned, product):
    rows, channels = mine.shape
    size_x = across.shape[0] - 2
    all_y, size_z = grad_z.shape[1:3]
    turned[...] = grad_z[:size_x].reshape(-1, channels).T
    taps = share_taps(rows, channels, spanned)
    for other, spot, value in products(across, turned, (size_x, all_y, size_z, channels), taps):
        product[other, spot] = (partial[other, spot] + value).T
    for other in range(4):
        offset = pl.multiple_of(taps[other][0], 16)
        share = product[other, pl.ds(offset, rows)] * (1.0 / voxels)
        if other == 0:
            mine[...] = share
        elif other == 3:
            later[...] = share
        elif other == 2:
            ahead[...] = share.astype(ahead.dtype)
        else:
            direct[...] = share.astype(direct.dtype)


def feature_kernel(
    grad, grad_z, kernel, rest, root, features, gamma, block,
    grad_features, mine, theirs, wide, shifted,
):
    size_x, size_y, size_z, channels = features.shape
    voxels = size_x * size_y * size_z
    gy = lax.axis_index("gy")
    spot = (pl.ds(0, size_x + 2), pl.ds(2, 2 * size_y))
    wide[spot + (pl.ds(EDGE, size_z),)] = grad[...].astype(F32)
    z_edges(wide, spot, grad_z[...], size_z)
    blank = jnp.zeros((size_x + 2, 2) + wide.shape[2:], F32)
    wide[:, :2] = blank
    wide[:, 2 + 2 * size_y :] = blank
    for number in range(5):
        start = EDGE - (number - 2)
        shifted[:, :, :, number * channels : (number + 1) * channels] = wide[
            :, pl.ds(gy * size_y, size_y + 4), start : start + size_z, :
        ].astype(BF16)

    def transposed(first_x, layers, first_y, lines, taps, count):
        patch = shifted[
            first_x : first_x + layers, first_y : first_y + lines, :, : count * channels
        ].reshape(-1, count * channels)
        rows = [jnp.concatenate([kernel[tap + k] for k in range(count)], axis=1) for tap in taps]
        weights = jnp.concatenate(rows, axis=0) if len(rows) > 1 else rows[0]
        out = lax.dot_general(
            patch, weights, (((1,), (1,)), ((), ())), preferred_element_type=F32
        )
        return out.reshape(layers, lines, size_z, len(taps) * channels)

    total = jnp.zeros((size_x, size_y, size_z, channels), F32)
    for along_y in range(5):
        pair = transposed(1, size_x + 1, 4 - along_y, size_y, (5 * along_y, 25 + 5 * along_y), 5)
        total = total + pair[1:, :, :, :channels] + pair[:-1, :, :, channels:]
    pair = transposed(0, size_x, 3, size_y + 1, (50, 55), 5)
    total = total + pair[:, 1:, :, :channels] + pair[:, :-1, :, channels:]
    total = total + transposed(0, size_x, 2, size_y, (60,), 2)
    total = total.reshape(voxels, channels)
    occupied = jnp.where(block[size_x:].astype(F32).reshape(voxels, channels) > 0.0, 1.0, 0.0)
    latent_grad = occupied * (total + rest[...].reshape(voxels, channels))
    inv_root = root[...]
    feats = features[...].astype(F32).reshape(voxels, channels)
    weighted = latent_grad * feats * inv_root * inv_root * inv_root
    coupled = lax.dot_general(
        weighted, gamma[...], (((1,), (1,)), ((), ())), precision=HIGHEST, preferred_element_type=F32
    )
    grad_features[...] = (latent_grad * inv_root - feats * coupled).astype(BF16).reshape(features.shape)
    factor = 0.5 / math.sqrt(voxels)
    sums = -factor * jnp.dot(
        (feats * feats).T, weighted, precision=HIGHEST, preferred_element_type=F32
    )
    ones = -factor * jnp.broadcast_to(jnp.sum(weighted, axis=0, keepdims=True), (8, channels))
    half = channels // 2
    first_z = lax.axis_index("gz") == 0
    mine[:half] = jnp.where(first_z, sums[:half], sums[half:])
    theirs[:half] = jnp.where(first_z, sums[half:], sums[:half])
    mine[half:] = ones
    theirs[half:] = ones


def join_kernel(mine, theirs, kept, direct, quarter, gamma, beta, share):
    share[...] = kept[...] + direct[...].astype(F32) + quarter[...].astype(F32)
    half = gamma.shape[0] // 2
    first_z = lax.axis_index("gz") == 0
    own, other = mine[:half], theirs[:half]
    gamma[:half] = jnp.where(first_z, own, other)
    gamma[half:] = jnp.where(first_z, other, own)
    beta[...] = mine[half : half + 1]


def call(body, outs, scratch, args, far=()):
    spaces = [pltpu.HBM if n in far else pltpu.VMEM for n in range(len(args))]
    args = [pltpu.with_memory_space_constraint(a, space) for a, space in zip(args, spaces)]
    return pl.pallas_call(
        body,
        out_shape=outs,
        in_specs=[pl.BlockSpec(memory_space=space) for space in spaces],
        out_specs=[pl.BlockSpec(memory_space=pltpu.VMEM)] * len(outs),
        scratch_shapes=scratch,
        compiler_params=pltpu.CompilerParams(vmem_limit_bytes=24 << 20),
    )(*args)


def fast_local(features, scales, occupancy, kernel, gamma, beta):
    shape = features.shape
    size_x, size_y, size_z, channels = shape
    voxels = size_x * size_y * size_z
    rest_of = shape[1:]
    latent, across_y, first_x, second_x, root, kept_features, kept_gamma = call(
        latent_kernel,
        [
            pltpu.VMEM(shape, BF16),
            pltpu.VMEM((2 * size_x,) + rest_of, BF16),
            pltpu.VMEM((4,) + rest_of, BF16),
            pltpu.VMEM((4,) + rest_of, BF16),
            pltpu.VMEM((voxels, channels), F32),
            pltpu.VMEM(shape, BF16),
            pltpu.VMEM(gamma.shape, F32),
        ],
        [
            pltpu.VMEM(shape, BF16),
            pltpu.VMEM((1, channels), F32),
            pltpu.SMEM(occupancy.shape, jnp.int32),
            pltpu.SemaphoreType.DMA((5,)),
        ],
        (features, scales, occupancy, gamma, beta.reshape(1, channels)),
        (0, 1, 2, 3, 4),
    )
    middle = lambda x, z: (3 - x, z) if x in (1, 2) else (x, 1 - z)
    side = flipped(across_y, "gy")
    corner = exchanged(first_x, ("gx", "gy"), lambda x, y: (x ^ 1, 1 - y))
    first = exchanged(first_x, "gx", lambda x: (x ^ 1,))
    corner_2 = exchanged(
        second_x, ("gx", "gy", "gz"), lambda x, y, z: (3 - x, 1 - y, z) if x in (1, 2) else (x, y, 1 - z)
    )
    second = exchanged(second_x, ("gx", "gz"), middle)
    sent = (side, first, corner, second, corner_2)
    around = (across_y,) + sent + tuple(
        flipped(part, "gz") for part in (latent, side[:size_x]) + tuple(part[:2] for part in sent[1:])
    )
    wide_y = 2 * size_y + 4
    wide_z = size_z + 2 * EDGE
    kept_kernel, = call(
        load_kernel, [pltpu.VMEM(kernel.shape, BF16)], [pltpu.SemaphoreType.DMA((4,))], (kernel,), (0,)
    )
    grad, rest, wide = call(
        mean_kernel,
        [
            pltpu.VMEM((size_x + 2, 2 * size_y, size_z, channels), BF16),
            pltpu.VMEM(shape, F32),
            pltpu.VMEM((size_x + 4, wide_y, wide_z, channels), F32),
        ],
        [
            pltpu.VMEM((size_x + 4, wide_y, size_z, 5 * channels), BF16),
            pltpu.VMEM((size_x + 2, 2 * size_y, size_z, channels), F32),
            pltpu.VMEM((size_x, 2 * size_y, size_z, channels), F32),
        ],
        around + (kept_kernel,),
    )
    grad_z = flipped(grad, "gz")
    rows = 62 * channels // 16
    spanned = 5
    turned = pltpu.VMEM((channels, 2 * voxels), BF16)
    pieces = (4, spanned * channels, channels)
    partial, across = call(
        functools.partial(partial_kernel, spanned, rows),
        [pltpu.VMEM(pieces, F32), pltpu.VMEM((size_x + 2, wide_y, wide_z, channels), F32)],
        [turned],
        around + (grad, wide),
    )
    mine, later, ahead, direct = call(
        functools.partial(share_kernel, spanned, voxels),
        [pltpu.VMEM((rows, channels), F32)] * 2 + [pltpu.VMEM((rows, channels), BF16)] * 2,
        [turned, pltpu.VMEM(pieces, F32)],
        (partial, across, grad_z),
    )
    ahead = exchanged(ahead, "gx", lambda x: (x ^ 1,))
    direct = exchanged(direct, "gx", lambda x: (x ^ 1,))
    grad_features, sums, others = call(
        feature_kernel,
        [jax.ShapeDtypeStruct(shape, BF16)] + [pltpu.VMEM((channels // 2 + 8, channels), F32)] * 2,
        [
            pltpu.VMEM((size_x + 2, wide_y, wide_z, channels), F32),
            pltpu.VMEM((size_x + 2, size_y + 4, size_z, 5 * channels), BF16),
        ],
        (grad, grad_z, kept_kernel, rest, root, kept_features, kept_gamma, across_y),
    )
    sums = sums + flipped(others, "gz")
    quarter = exchanged((later + ahead.astype(F32)).astype(BF16), "gx", lambda x: (3 - x,))
    sums = sums + flipped(sums, "gy")
    near = exchanged(sums, "gx", lambda x: (x ^ 1,))
    second_near = exchanged(sums, "gx", lambda x: (x ^ 2,))
    mirrored = exchanged(sums, "gx", lambda x: (3 - x,))
    sums = (sums + near) + (second_near + mirrored)
    struct = jax.ShapeDtypeStruct
    grad_gamma, grad_beta, share = call(
        join_kernel,
        [struct((channels, channels), F32), struct((1, channels), F32), struct((rows, channels), F32)],
        [],
        (sums, flipped(sums, "gz"), mine, direct, quarter),
    )
    return grad_features, share.reshape(-1), grad_gamma, grad_beta.reshape(channels)


def chosen(features, scales, occupancy, kernel, gamma, beta):
    sizes = tuple(lax.axis_size(axis) for axis in ("gx", "gy", "gz"))
    size_x, size_y, size_z, channels = features.shape
    small = size_x >= 2 and size_y >= 2 and size_z % 16 == 0 and size_x * size_y * size_z <= 1024
    if sizes == (4, 2, 2) and small and channels == 128:
        return fast_local(features, scales, occupancy, kernel, gamma, beta)
    return local(features, scales, occupancy, kernel, gamma, beta)


def solution(mesh):
    step = jax.shard_map(
        chosen,
        mesh=mesh,
        in_specs=(
            P(("groups", "gx"), "gy", "gz", None),
            P(("groups", "gx"), "gy", "gz", None),
            P(("groups", "gx"), "gy", "gz"),
            P(),
            P(),
            P(),
        ),
        out_specs=(
            P(("groups", "gx"), "gy", "gz", None),
            P(("groups", "gx", "gy", "gz")),
            P("groups", None),
            P("groups"),
        ),
        check_vma=False,
    )
    if tuple(mesh.shape[axis] for axis in ("gx", "gy", "gz")) != (4, 2, 2):
        return step
    return step
```
